256 devices in a mesh: tm: 128 (over z, y, x), rows: 2 (over core).
Axes of the slice: x: 4, y: 4, z: 8, core: 2. Of those that a mesh axis runs over, the one named last changes fastest.
Arguments:
- site_rates: float32 [256], replicated, may hold values from 0.0005 to 0.2
- prior_mean: float32 [512, 384], replicated, may hold values from -6 to 6
- observed: float32 [128, 256, 384], P('tm'), may hold values from -6 to 6
- obs_mask: int32 [128, 256], P('tm'), may hold values 0 or 1
- filter_gains: float32 [128, 512, 256], P('tm', 'rows'), may hold values from -0.05 to 0.8, as said below
- smooth_gains: float32 [128, 512, 512], P('tm', 'rows'), may hold values from -0.02 to 1, as said below
Outputs:
- filtered: float32 [128, 512, 384], P('tm', 'rows')
- smoothed: float32 [128, 512, 384], P('tm', 'rows')
The draws below stay inside these ranges and needn't reach their ends.
Inputs may be any that keep to these rules, and one draw needn't show every extreme that they name: `filter_gains`: gain of each step; row 2i + c is component c of site i, column j a site. `smooth_gains`: smoother gain of each step; rows and columns are state entries.
All inputs are finite; a program needn't handle non-finite values. No bound on the sum of `obs_mask` on one device may be relied on, other than what follows from the above.
Results may differ from the reference program's by a relative error of at most 0.0003.
Values sent between devices are 32-bit elements; how exact they have to be, the bound alone decides.
A program may use at most 128 MiB of HBM per device.

```python
import math
import jax
import jax.numpy as jnp
from jax import lax

SITES = 256
STATE = 512
PATHS = 384
TIME_STEPS = 128


def draw_filter_gains(key, part):
    noise_random_key, gain_key = jax.random.split(key)
    shape = (TIME_STEPS, STATE, SITES)
    noise = jnp.clip(jax.random.normal(noise_random_key, shape, jnp.float32), -4.0, 4.0)
    level = jnp.exp(jax.random.uniform(gain_key, shape, jnp.float32, math.log(0.2), math.log(0.8)))
    row_ids = jnp.arange(STATE)[:, None]
    col_ids = jnp.arange(SITES)[None, :]
    own_site = row_ids // 2 == col_ids
    diagonal_entries = jnp.where(row_ids % 2 == 0, level, 0.02 * level)
    return jnp.where(own_site[None], diagonal_entries, noise * (0.06 / math.sqrt(SITES))).astype(jnp.float32)


def draw_smooth_gains(key, part):
    rate_key = jax.random.fold_in(key, 7)
    location_key = jax.random.fold_in(key, 11)
    noise_random_key, perturbation_key, spike_random_key = jax.random.split(key, 3)
    shape = (TIME_STEPS, STATE, STATE)
    damping_rates = jnp.exp(jax.random.uniform(rate_key, (1, STATE), jnp.float32, math.log(0.0005), math.log(0.1)))
    noise = jnp.clip(jax.random.normal(noise_random_key, shape, jnp.float32), -4.0, 4.0)
    small_perturbation = jax.random.uniform(perturbation_key, (TIME_STEPS, STATE), jnp.float32, 0.5, 1.5)
    spike_time_steps = jax.random.randint(location_key, (3,), 0, TIME_STEPS)
    spike_extent = jax.random.uniform(spike_random_key, (3,), jnp.float32, 0.5, 0.8)
    spike_hits = jnp.arange(TIME_STEPS)[:, None] == spike_time_steps[None, :]
    spike_multiplier = jnp.prod(jnp.where(spike_hits, spike_extent[None, :], 1.0), axis=1, keepdims=True)
    diagonal_entries = jnp.exp(-damping_rates * small_perturbation) * spike_multiplier
    identity = jnp.arange(STATE)[:, None] == jnp.arange(STATE)[None, :]
    return jnp.where(identity[None], diagonal_entries[:, :, None], noise * (0.03 / math.sqrt(STATE))).astype(jnp.float32)


def touch_ends(result, rng, smallest, top_value):
    shape = result.shape
    place = [jax.random.randint(jax.random.fold_in(rng, axis), (), 0, shape[axis]) for axis in range(len(shape))]
    result = result.at[tuple(place)].set(smallest)
    longest = shape.index(max(shape))
    place[longest] = (place[longest] + 1) % shape[longest]
    return result.at[tuple(place)].set(top_value)


def level_of(key, dims, shards, least, high):
    def one(dim, blocks):
        steps = jax.random.uniform(jax.random.fold_in(jax.random.fold_in(key, 6), dim), (blocks,), jnp.float32, least / len(shards), high / len(shards))
        return jnp.repeat(jnp.exp(steps), dims[dim] // blocks).reshape((-1,) + (1,) * (len(dims) - dim - 1))

    gain = one(*shards[0])
    for cut in shards[1:]:
        gain = gain * one(*cut)
    return gain


def scatter_about(stream_key, dims, scale, limit, cuts=(), kind=jnp.bfloat16):
    drawn = scale * jax.random.normal(stream_key, dims, jnp.float32)
    if cuts:
        drawn = drawn * level_of(stream_key, dims, cuts, -0.22, 0.18)
    return jnp.clip(drawn, -limit, limit).astype(kind)


def setup_inputs(seed: int = 0) -> dict:
    arg_keys = jax.random.split(jax.random.key(seed), 7)
    site_rates = jnp.clip(jnp.exp(jax.random.uniform(arg_keys[0], (SITES,), jnp.float32, math.log(0.0005), math.log(0.2))), 0.0005, 0.2)
    prior_mean = scatter_about(arg_keys[1], (STATE, PATHS), 1.0, 6.0, (), jnp.float32)
    observed = scatter_about(arg_keys[2], (TIME_STEPS, SITES, PATHS), 1.0, 6.0, ((0, 128),), jnp.float32)
    obs_mask = touch_ends((jax.random.randint(arg_keys[3], (TIME_STEPS, SITES), 0, 2) < 1).astype(jnp.int32), jax.random.fold_in(arg_keys[3], 1), 0, 1)
    filter_gains = draw_filter_gains(jax.random.fold_in(arg_keys[6], 71), 0)
    smooth_gains = draw_smooth_gains(jax.random.fold_in(arg_keys[6], 71), 0)
    return {"site_rates": site_rates, "prior_mean": prior_mean, "observed": observed, "obs_mask": obs_mask, "filter_gains": filter_gains, "smooth_gains": smooth_gains}


def product(left, right):
    return jnp.dot(left, right, precision=lax.Precision.HIGHEST, preferred_element_type=jnp.float32)


def transition_blocks(site_rates):
    decay = jnp.exp(-site_rates)
    top = jnp.stack([decay * (1.0 + site_rates), decay], -1)
    bottom = jnp.stack([-decay * site_rates * site_rates, decay * (1.0 - site_rates)], -1)
    return jnp.stack([top, bottom], 1)


def apply_transition(values, site_rates):
    blocks = transition_blocks(site_rates)
    paired = values.reshape(site_rates.shape[0], 2, values.shape[-1])
    moved = jnp.einsum("scd,sdb->scb", blocks, paired, precision=lax.Precision.HIGHEST)
    return moved.reshape(values.shape)


def reference(site_rates, prior_mean, observed, obs_mask, filter_gains, smooth_gains):
    def forward(state_now, inputs):
        obs_step, mask_step, gain_step = inputs
        predicted = apply_transition(state_now, site_rates)
        values = predicted.reshape(SITES, 2, predicted.shape[-1])[:, 0, :]
        innovation = mask_step.astype(jnp.float32)[:, None] * (obs_step - values)
        updated = predicted + product(gain_step, innovation)
        return updated, updated

    _, filtered = lax.scan(forward, prior_mean, (observed, obs_mask, filter_gains))

    def backward(later, inputs):
        state_step, gain_step = inputs
        updated = state_step + product(gain_step, later - apply_transition(state_step, site_rates))
        return updated, updated

    _, earlier = lax.scan(backward, filtered[-1], (filtered[:-1], smooth_gains[:-1]), reverse=True)
    smoothed = jnp.concatenate([earlier, filtered[-1:]], 0)
    return (filtered, smoothed)
```

```python
import functools

import jax
import jax.numpy as jnp
from jax import lax
from jax.experimental import pallas as pl
from jax.experimental.pallas import tpu as pltpu
from jax.sharding import PartitionSpec as P

F32, BF16 = jnp.float32, jnp.bfloat16
SIDE = 4
STEPS = SIDE * SIDE
LANE = 128
PAD = 16


def halves(value):
    high = value.astype(BF16)
    return high, (value - high.astype(F32)).astype(BF16)


def product(left, right):
    dot = functools.partial(jnp.dot, preferred_element_type=F32)
    left_high, left_low = halves(left)
    right_high, right_low = halves(right)
    rows = left.shape[0]
    both = dot(jnp.concatenate([left_high, left_low], 0), right_high)
    return both[:rows] + (both[rows:] + dot(left_high, right_low))


class Place:
    def __init__(self, blocks):
        time = lax.axis_index("tm")
        self.blocks = blocks
        self.z, self.q = lax.div(time, STEPS), lax.rem(time, STEPS)
        self.y, self.x = lax.div(self.q, SIDE), lax.rem(self.q, SIDE)
        self.core = lax.axis_index("rows")
        self.partner = {"tm": time, "rows": 1 - self.core}

    def chip(self, dy, dx):
        return lax.rem(self.y + dy % SIDE, SIDE) * SIDE + lax.rem(self.x + dx % SIDE, SIDE)

    def device(self, q, core):
        return {"tm": self.z * STEPS + q, "rows": core}

    def above(self, dz):
        z = lax.rem(self.z + dz % self.blocks, self.blocks)
        return {"tm": z * STEPS + self.q, "rows": self.core}


def remote(src, dst, send, recv, device):
    return pltpu.make_async_remote_copy(
        src_ref=src, dst_ref=dst, send_sem=send, recv_sem=recv, device_id=device, device_id_type=pl.DeviceIdType.MESH
    )


def gather_plane(place, own, buf, send, recv, side_send, side_recv, local):
    core, rows = place.core, own.shape[0]
    half, quarter = rows // 2, rows // 4
    axes = ((0, 1), (1, 0))
    started, index = {}, [0]

    def off(*terms):
        return tuple(sum(scale * axis[i] for scale, axis in terms) for i in (0, 1))

    def view(offset, start, size):
        return buf.at[place.chip(*offset), core, pl.ds(start, size)]

    def begin(key, offset, start, size, to, mine=False):
        src = own.at[pl.ds(start, size)] if mine else view(offset, start, size)
        i = index[0]
        index[0] += 1
        copy = remote(src, view(offset, start, size), send.at[i], recv.at[i], place.device(place.chip(*to), core))
        copy.start()
        started[key] = copy

    def across(offset, h):
        i = h * STEPS + (offset[0] % SIDE) * SIDE + offset[1] % SIDE
        mine = offset == (0, 0)
        src = own.at[pl.ds(h * half, half)] if mine else view(offset, h * half, half)
        copy = remote(src, view(offset, h * half, half), side_send.at[i], side_recv.at[i], place.partner)
        copy.start()
        started["side", i] = copy

    keep = pltpu.make_async_copy(own, buf.at[place.q, core], local)
    keep.start()
    for h in (0, 1):
        for s in (1, -1):
            begin(("a1", h, s), (0, 0), h * half, half, off((s, axes[h])), True)
    for h in (0, 1):
        for s in (1, -1):
            begin(("b1", h, 0, s), (0, 0), h * half, half, off((s, axes[1 - h])), True)
    for h in (0, 1):
        across((0, 0), h)
    yield
    for s in (1, -1):
        for h in (0, 1):
            a, b = axes[h], axes[1 - h]
            started["a1", h, s].wait_recv()
            came = off((-s, a))
            begin(("a2", h, s), came, h * half + (quarter if s < 0 else 0), quarter, off((s, a)))
            for t in (1, -1):
                begin(("b1", h, -s, t), came, h * half, half, off((t, b)))
            across(came, h)
            yield

    def second(h, o, s):
        a, b = axes[h], axes[1 - h]
        started["b1", h, o, s].wait_recv()
        came = off((o, a), (-s, b))
        begin(("b2", h, o, s), came, h * half + (quarter if s < 0 else 0), quarter, off((s, b)))
        across(came, h)

    for s in (1, -1):
        for h in (0, 1):
            second(h, 0, s)
            yield
    for h in (0, 1):
        for s in (1, -1):
            started["a2", h, s].wait_recv()
        came = off((2, axes[h]))
        for t in (1, -1):
            begin(("b1", h, 2, t), came, h * half, half, off((t, axes[1 - h])))
        across(came, h)
        yield
    for o in (-1, 1, 2):
        for s in (1, -1):
            for h in (0, 1):
                second(h, o, s)
                yield
    for o in (0, -1, 1, 2):
        for h in (0, 1):
            for s in (1, -1):
                started["b2", h, o, s].wait_recv()
            across(off((o, axes[h]), (2, axes[1 - h])), h)
            yield
    for i in range(2 * STEPS):
        started["side", i].wait_recv()
    keep.wait()
    for copy in started.values():
        copy.wait_send()
    yield


def gather_rows(place, stage, buf, send, recv, side_send, side_recv, local):
    core = place.core
    keep = pltpu.make_async_copy(stage, buf.at[place.q, core], local)
    keep.start()
    copies, sides = [], []
    order = sorted(range(1, STEPS), key=lambda i: -sum(min(k, SIDE - k) for k in divmod(i, SIDE)))
    for i in order:
        copy = remote(stage, buf.at[place.q, core], send.at[i], recv.at[i],
                      place.device(place.chip(*divmod(i, SIDE)), core))
        copy.start()
        copies.append(copy)

    def across(i, src):
        dy, dx = divmod(i, SIDE)
        dst = buf.at[place.chip(-dy, -dx), core]
        copy = remote(dst if src is None else src, dst, side_send.at[i], side_recv.at[i], place.partner)
        copy.start()
        sides.append(copy)

    across(0, stage)
    for i, copy in reversed(list(zip(order, copies))):
        copy.wait_recv()
        across(i, None)
    for copy in sides:
        copy.wait_recv()
    keep.wait()
    for copy in copies + sides:
        copy.wait_send()


def kernel(blocks, gain, back, obs, prior, coef, filt, smooth,
           gains, backs, seen, kept, pmap, qmap, stage, enter, leave, turn, far, sout, fsend,
           ksend, krecv, kside_s, kside_r, gsend, grecv, gside_s, gside_r,
           osend, orecv, msend, mrecv, mside_s, mside_r, chain, fsem, ssem, local):
    place = Place(blocks)
    core = place.core
    barrier = pltpu.get_barrier_semaphore()
    greet = [place.partner, place.above(1), place.above(-1)]
    for i in range(1, STEPS):
        q = place.chip(*divmod(i, SIDE))
        greet += [place.device(q, core), place.device(q, 1 - core)]
    for device in greet:
        pl.semaphore_signal(barrier, inc=1, device_id=device, device_id_type=pl.DeviceIdType.MESH)
    pl.semaphore_wait(barrier, len(greet))

    watch = []
    for i in range(1, STEPS):
        q = place.chip(*divmod(i, SIDE))
        copy = remote(obs.at[q, core], seen.at[place.q], osend.at[i], orecv.at[i], place.device(q, core))
        copy.start()
        watch.append(copy)
    own_obs = pltpu.make_async_copy(obs.at[place.q, core], seen.at[place.q], local.at[0])
    own_obs.start()

    first = gather_plane(place, gain, gains, ksend, krecv, kside_s, kside_r, local.at[1])
    for _ in first:
        pass
    for copy in watch:
        copy.wait()
    own_obs.wait()
    second = gather_plane(place, back, backs, gsend, grecv, gside_s, gside_r, local.at[2])
    next(second)

    alpha, beta = coef[0:1, :], coef[1:2, :]

    def moved(state):
        swap = jnp.concatenate([state[:, i * LANE:(i + 1) * LANE] for i in (1, 0, 3, 2)], 1)
        return alpha * state + beta * swap

    def values(state):
        return jnp.concatenate([state[:, :LANE], state[:, 2 * LANE:3 * LANE]], 1)

    row = lax.broadcasted_iota(jnp.int32, (PAD, 4 * LANE), 0)
    lane = lax.broadcasted_iota(jnp.int32, (PAD, 4 * LANE), 1)
    unit = jnp.where(lane == row + (place.q * 2 + core) * PAD, 1.0, 0.0).astype(F32)
    zero = jnp.zeros((PAD, 4 * LANE), F32)

    def forward(k, state, rows):
        predicted = moved(state)
        target = seen[k]
        if rows > PAD:
            target = jnp.concatenate([target, jnp.zeros((rows - PAD, 2 * LANE), F32)], 0)
        innovation = target - values(predicted)
        return predicted + jnp.concatenate([product(innovation, gains[k, half]) for half in (0, 1)], 1)

    both = lax.fori_loop(0, STEPS, lambda k, state: forward(k, state, 2 * PAD), jnp.concatenate([zero, unit], 0))
    stage[...] = both[PAD:]
    leave[...] = both[:PAD]
    for _ in second:
        pass
    gather_rows(place, stage, pmap, msend.at[0], mrecv.at[0], mside_s.at[0], mside_r.at[0], local.at[3])

    def mapped(state, table):
        return product(state, table[...].reshape(4 * LANE, 4 * LANE))

    up = remote(leave, enter, chain.at[0], chain.at[1], place.above(1))

    @pl.when(place.z == 0)
    def _():
        enter[...] = prior[...]

    @pl.when(place.z > 0)
    def _():
        up.wait_recv()

    @pl.when(place.z < blocks - 1)
    def _():
        leave[...] = leave[...] + mapped(enter[...], pmap)
        up.start()

    def hand_on(value_ref, k, out, sem):
        for half in (0, 1):
            part = value_ref.at[k, half]
            home = jnp.logical_and(k == place.q, core == half)

            @pl.when(home)
            def _():
                pltpu.make_async_copy(part, out.at[place.q, core], sem.at[1]).start()

            @pl.when(jnp.logical_not(home))
            def _():
                remote(part, out.at[place.q, core], sem.at[0], sem.at[1], place.device(k, half)).start()

    def all_handed(out, sem):
        pltpu.make_async_copy(out, out, sem.at[1]).wait()
        rest = out.at[pl.ds(0, STEPS - 1)]
        pltpu.make_async_copy(rest, rest, sem.at[0]).wait()
        pltpu.make_async_copy(out.at[0, 0], out.at[0, 0], sem.at[0]).wait()

    def filter_step(k, state):
        state = forward(k, state, PAD)
        kept[k] = state
        fsend[k, 0] = state[:, :2 * LANE]
        fsend[k, 1] = state[:, 2 * LANE:]
        hand_on(fsend, k, filt, fsem)
        return state

    lax.fori_loop(0, STEPS, filter_step, enter[...])

    @pl.when(place.z < blocks - 1)
    def _():
        up.wait_send()

    def smoothed(k, ahead):
        wanted = ahead - moved(kept[k])
        return kept[k] + back_product(k, wanted)

    def back_product(k, value):
        return jnp.concatenate([product(value, backs[k, half]) for half in (0, 1)], 1)

    def both_back(i, state):
        k = STEPS - 1 - i
        held = kept[k]
        wanted = jnp.concatenate([state[:PAD] - moved(held), state[PAD:]], 0)
        return jnp.concatenate([held, zero], 0) + back_product(k, wanted)

    both = lax.fori_loop(0, STEPS, both_back, jnp.concatenate([zero, unit], 0))
    turn[...] = both[PAD:]
    far[0] = both[:PAD]
    gather_rows(place, turn, qmap, msend.at[1], mrecv.at[1], mside_s.at[1], mside_r.at[1], local.at[4])

    down = remote(far.at[0], far.at[1], chain.at[2], chain.at[3], place.above(-1))

    @pl.when(place.z == blocks - 1)
    def _():
        far[1] = zero

    @pl.when(place.z < blocks - 1)
    def _():
        down.wait_recv()

    @pl.when(place.z > 0)
    def _():
        far[0] = far[0] + mapped(far[1], qmap)
        down.start()

    def smooth_step(i, state):
        k = STEPS - 1 - i
        state = smoothed(k, state)
        sout[k, 0] = state[:, :2 * LANE]
        sout[k, 1] = state[:, 2 * LANE:]
        hand_on(sout, k, smooth, ssem)
        return state

    lax.fori_loop(0, STEPS, smooth_step, far[1])

    @pl.when(place.z > 0)
    def _():
        down.wait_send()

    all_handed(filt, fsem)
    all_handed(smooth, ssem)


def transition_blocks(site_rates):
    decay = jnp.exp(-site_rates)
    top = jnp.stack([decay * (1.0 + site_rates), decay], -1)
    bottom = jnp.stack([-decay * site_rates * site_rates, decay * (1.0 - site_rates)], -1)
    return jnp.stack([top, bottom], 1)


def state_order(rows):
    return rows.reshape(2, LANE, 2, -1).transpose(0, 2, 1, 3).reshape(4 * LANE, -1)


def body(site_rates, prior_mean, observed, obs_mask, filter_gains, smooth_gains):
    time_count, time_index = lax.axis_size("tm"), lax.axis_index("tm")
    blocks = time_count // STEPS
    core = lax.axis_index("rows")
    paths = prior_mean.shape[1]
    share = paths // (2 * STEPS)
    table = transition_blocks(site_rates)
    alpha = state_order(jnp.stack([table[:, 0, 0], table[:, 1, 1]], 1).reshape(-1, 1)).T
    beta = state_order(jnp.stack([table[:, 0, 1], table[:, 1, 0]], 1).reshape(-1, 1)).T
    coef = jnp.concatenate([alpha, beta, jnp.zeros((6, 4 * LANE), F32)], 0)
    gain = filter_gains[0] * obs_mask[0].astype(F32)[None, :]
    gain = gain.reshape(LANE, 2, 2 * LANE).transpose(2, 1, 0).reshape(2 * LANE, 2 * LANE)
    back = jnp.where(time_index == time_count - 1, 0.0, smooth_gains[0])
    back = back.reshape(LANE, 2, 2, LANE, 2).transpose(2, 4, 3, 1, 0).reshape(4 * LANE, 2 * LANE)
    pad = ((0, 0), (0, PAD - share), (0, 0))
    obs = jnp.pad(observed[0].T.reshape(2 * STEPS, share, 2 * LANE), pad).reshape(STEPS, 2, PAD, 2 * LANE)
    mine = (lax.rem(time_index, STEPS) * 2 + core) * share
    prior = state_order(lax.dynamic_slice_in_dim(prior_mean, mine, share, 1)).T
    prior = jnp.pad(prior, ((0, PAD - share), (0, 0)))

    vmem = pl.BlockSpec(memory_space=pltpu.VMEM)
    dma, out = pltpu.SemaphoreType.DMA, jax.ShapeDtypeStruct((STEPS, 2, PAD, 2 * LANE), F32)
    filt, smooth = pl.pallas_call(
        functools.partial(kernel, blocks),
        out_shape=(out, out),
        in_specs=[vmem] * 5,
        out_specs=(vmem, vmem),
        scratch_shapes=[
            pltpu.VMEM((STEPS, 2, 2 * LANE, 2 * LANE), F32),
            pltpu.VMEM((STEPS, 2, 4 * LANE, 2 * LANE), F32),
            pltpu.VMEM((STEPS, PAD, 2 * LANE), F32),
            pltpu.VMEM((STEPS, PAD, 4 * LANE), F32),
            pltpu.VMEM((STEPS, 2, PAD, 4 * LANE), F32),
            pltpu.VMEM((STEPS, 2, PAD, 4 * LANE), F32),
            pltpu.VMEM((PAD, 4 * LANE), F32),
            pltpu.VMEM((PAD, 4 * LANE), F32),
            pltpu.VMEM((PAD, 4 * LANE), F32),
            pltpu.VMEM((PAD, 4 * LANE), F32),
            pltpu.VMEM((2, PAD, 4 * LANE), F32),
            pltpu.VMEM((STEPS, 2, PAD, 2 * LANE), F32),
            pltpu.VMEM((STEPS, 2, PAD, 2 * LANE), F32),
            dma((40,)), dma((40,)), dma((32,)), dma((32,)),
            dma((40,)), dma((40,)), dma((32,)), dma((32,)),
            dma((STEPS,)), dma((STEPS,)),
            dma((2, STEPS)), dma((2, STEPS)), dma((2, STEPS)), dma((2, STEPS)),
            dma((4,)), dma((2,)), dma((2,)), dma((5,)),
        ],
        compiler_params=pltpu.CompilerParams(
            collective_id=0, has_side_effects=True, vmem_limit_bytes=60 * 1024 * 1024
        ),
        name="two_level_scan",
    )(gain, back, obs, prior, coef)

    def placed(value):
        rows = value.reshape(2 * STEPS, PAD, 2 * LANE)[:, :share].reshape(paths, 2, LANE)
        return rows.transpose(2, 1, 0).reshape(1, 2 * LANE, paths)

    return placed(filt), placed(smooth)


def solution(mesh):
    placed = (
        P(),
        P(),
        P("tm", None, None),
        P("tm", None),
        P("tm", "rows", None),
        P("tm", "rows", None),
    )
    return jax.shard_map(
        body,
        mesh=mesh,
        in_specs=placed,
        out_specs=(P("tm", "rows", None), P("tm", "rows", None)),
        check_vma=False,
    )
```

```python
import functools

import jax
import jax.numpy as jnp
from jax import lax
from jax.experimental import pallas as pl
from jax.experimental.pallas import tpu as pltpu
from jax.sharding import PartitionSpec as P

F32, BF16 = jnp.float32, jnp.bfloat16
SIDE = 4
STEPS = SIDE * SIDE
LANE = 128
PAD = 16


def halves(value):
    high = value.astype(BF16)
    return high, (value - high.astype(F32)).astype(BF16)


def product(left, right):
    dot = functools.partial(jnp.dot, preferred_element_type=F32)
    left_high, left_low = halves(left)
    right_high, right_low = halves(right)
    rows = left.shape[0]
    both = dot(jnp.concatenate([left_high, left_low], 0), right_high)
    return both[:rows] + (both[rows:] + dot(left_high, right_low))


class Place:
    def __init__(self, blocks):
        time = lax.axis_index("tm")
        self.blocks = blocks
        self.z, self.q = lax.div(time, STEPS), lax.rem(time, STEPS)
        self.y, self.x = lax.div(self.q, SIDE), lax.rem(self.q, SIDE)
        self.core = lax.axis_index("rows")
        self.partner = {"tm": time, "rows": 1 - self.core}

    def chip(self, dy, dx):
        return lax.rem(self.y + dy % SIDE, SIDE) * SIDE + lax.rem(self.x + dx % SIDE, SIDE)

    def device(self, q, core):
        return {"tm": self.z * STEPS + q, "rows": core}

    def above(self, dz):
        z = lax.rem(self.z + dz % self.blocks, self.blocks)
        return {"tm": z * STEPS + self.q, "rows": self.core}


def remote(src, dst, send, recv, device):
    return pltpu.make_async_remote_copy(
        src_ref=src, dst_ref=dst, send_sem=send, recv_sem=recv, device_id=device, device_id_type=pl.DeviceIdType.MESH
    )


class Gather:
    def __init__(self, place, own, buf, send, recv, side_send, side_recv, local):
        self.place, self.own, self.buf = place, own, buf
        self.half, self.quarter = own.shape[0] // 2, own.shape[0] // 4
        self.sems, self.side_sems = (send, recv), (side_send, side_recv)
        self.keep = pltpu.make_async_copy(own, buf.at[place.q, place.core], local)
        signs, sides = (1, -1), (0, 1)
        keys = [("a1", h, s) for h in sides for s in signs] + [("a2", h, s) for h in sides for s in signs]
        keys += [(name, h, o, s) for name in ("b1", "b2") for h in sides for o in (0, -1, 1, 2) for s in signs]
        self.keys = {key: i for i, key in enumerate(keys)}

    @staticmethod
    def off(h, along, across=0):
        return ((across, along), (along, across))[h]

    def copy(self, key):
        name, h, s = key[0], key[1], key[-1]
        start, size = h * self.half, self.half
        if name == "a1":
            offset, to = (0, 0), self.off(h, s)
        elif name == "a2":
            offset, to = self.off(h, -s), self.off(h, s)
        elif name == "b1":
            offset, to = self.off(h, key[2]), self.off(h, 0, s)
        else:
            offset, to = self.off(h, key[2], -s), self.off(h, 0, s)
        if name in ("a2", "b2"):
            start, size = start + (self.quarter if s < 0 else 0), self.quarter
        place, i = self.place, self.keys[key]
        dst = self.buf.at[place.chip(*offset), place.core, pl.ds(start, size)]
        src = self.own.at[pl.ds(start, size)] if offset == (0, 0) else dst
        return remote(src, dst, self.sems[0].at[i], self.sems[1].at[i], place.device(place.chip(*to), place.core))

    def across(self, h, offset):
        place, dy, dx = self.place, offset[0] % SIDE, offset[1] % SIDE
        i = h * STEPS + dy * SIDE + dx
        part = pl.ds(h * self.half, self.half)
        dst = self.buf.at[place.chip(dy, dx), place.core, part]
        src = self.own.at[part] if (dy, dx) == (0, 0) else dst
        return remote(src, dst, self.side_sems[0].at[i], self.side_sems[1].at[i], place.partner)

    def begin(self):
        for name, rest in (("a1", ()), ("b1", (0,))):
            for h in (0, 1):
                for s in (1, -1):
                    self.copy((name, h, *rest, s)).start()
        for h in (0, 1):
            self.across(h, (0, 0)).start()
        self.keep.start()

    def relay(self, h, o, s):
        self.copy(("b1", h, o, s)).wait_recv()
        self.copy(("b2", h, o, s)).start()
        self.across(h, self.off(h, o, -s)).start()

    def stage(self, number):
        if number == 0:
            for s in (1, -1):
                for h in (0, 1):
                    self.copy(("a1", h, s)).wait_recv()
                    self.copy(("a2", h, s)).start()
                    for t in (1, -1):
                        self.copy(("b1", h, -s, t)).start()
                    self.across(h, self.off(h, -s)).start()
        if number == 1:
            for s in (1, -1):
                for h in (0, 1):
                    self.relay(h, 0, s)
            for h in (0, 1):
                for s in (1, -1):
                    self.copy(("a2", h, s)).wait_recv()
                for t in (1, -1):
                    self.copy(("b1", h, 2, t)).start()
                self.across(h, self.off(h, 2)).start()
        if number in (2, 3):
            for o in ((-1, 1), (2,))[number - 2]:
                for s in (1, -1):
                    for h in (0, 1):
                        self.relay(h, o, s)

    def finish(self):
        for o in (0, -1, 1, 2):
            for h in (0, 1):
                for s in (1, -1):
                    self.copy(("b2", h, o, s)).wait_recv()
                self.across(h, self.off(h, o, 2)).start()
        for i in range(STEPS):
            for h in (0, 1):
                self.across(h, divmod(i, SIDE)).wait()
        self.keep.wait()
        for key in self.keys:
            self.copy(key).wait_send()


class GatherRows:
    def __init__(self, place, own, buf, send, recv, side_send, side_recv, local):
        self.place, self.own, self.buf = place, own, buf
        self.sems, self.side_sems = (send, recv), (side_send, side_recv)
        self.keep = pltpu.make_async_copy(own, buf.at[place.q, place.core], local)
        self.order = sorted(range(1, STEPS), key=lambda i: -sum(min(k, SIDE - k) for k in divmod(i, SIDE)))

    def copy(self, i):
        place, (dy, dx) = self.place, divmod(i, SIDE)
        to = place.device(place.chip(dy, dx), place.core)
        return remote(self.own, self.buf.at[place.q, place.core], self.sems[0].at[i], self.sems[1].at[i], to)

    def across(self, i):
        place, (dy, dx) = self.place, divmod(i, SIDE)
        dst = self.buf.at[place.chip(-dy, -dx), place.core]
        return remote(dst if i else self.own, dst, self.side_sems[0].at[i], self.side_sems[1].at[i], place.partner)

    def begin(self):
        for i in self.order:
            self.copy(i).start()
        self.across(0).start()
        self.keep.start()

    def finish(self):
        for i in reversed(self.order):
            self.copy(i).wait_recv()
            self.across(i).start()
        for i in range(STEPS):
            self.across(i).wait()
        self.keep.wait()
        for i in self.order:
            self.copy(i).wait_send()


def turned(ref, i, start):
    return ref[i, pl.ds(start, LANE, stride=2), :].T


def kernel(blocks, rates, mask, gain_rows, watched, back_hbm, start_hbm, filt_rows, smooth_rows,
           gain, back, mid, back_rows, start_rows, woven, spread, obs, prior, filt, smooth,
           gains, backs, seen, kept, pmap, qmap, stage, enter, leave, turn, far, sout, fsend,
           ksend, krecv, kside_s, kside_r, gsend, grecv, gside_s, gside_r,
           osend, orecv, msend, mrecv, mside_s, mside_r, chain, fsem, ssem, local):
    place = Place(blocks)
    core = place.core
    share = watched.shape[1] // (2 * STEPS)
    paths = watched.shape[1]
    barrier = pltpu.get_barrier_semaphore()
    greet = [place.partner, place.above(1), place.above(-1)]
    for i in range(1, STEPS):
        q = place.chip(*divmod(i, SIDE))
        greet += [place.device(q, core), place.device(q, 1 - core)]
    for device in greet:
        pl.semaphore_signal(barrier, inc=1, device_id=device, device_id_type=pl.DeviceIdType.MESH)
    loads = []
    for i in range(4):
        loads.append(pltpu.make_async_copy(back_hbm.at[:, pl.ds(i * LANE, LANE)], back_rows.at[i], local.at[5 + i]))
    for i in range(paths // LANE):
        loads.append(pltpu.make_async_copy(start_hbm.at[:, pl.ds(i * LANE, LANE)], start_rows.at[i], local.at[9 + i]))
    for load in loads:
        load.start()

    kept_gain = gain_rows[...] * mask[...].astype(F32)
    for i in (0, 1):
        mid[i, pl.ds(0, 2 * LANE), :] = kept_gain[:, i * LANE:(i + 1) * LANE]
        for comp in (0, 1):
            gain[i * LANE:(i + 1) * LANE, comp * LANE:(comp + 1) * LANE] = turned(mid, i, comp)
    pl.semaphore_wait(barrier, len(greet))
    first = Gather(place, gain, gains, ksend, krecv, kside_s, kside_r, local.at[1])
    second = Gather(place, back, backs, gsend, grecv, gside_s, gside_r, local.at[2])
    first.begin()

    sites = watched[...].T
    empty = jnp.zeros((PAD - share, 2 * LANE), F32)
    for i in range(2 * STEPS):
        obs[i // 2, i % 2] = jnp.concatenate([sites[i * share:(i + 1) * share], empty], 0)
    watch = []
    for i in range(1, STEPS):
        q = place.chip(*divmod(i, SIDE))
        copy = remote(obs.at[q, core], seen.at[place.q], osend.at[i], orecv.at[i], place.device(q, core))
        copy.start()
        watch.append(copy)
    own_obs = pltpu.make_async_copy(obs.at[place.q, core], seen.at[place.q], local.at[0])
    own_obs.start()

    for load in loads:
        load.wait()
    live = jnp.where(lax.axis_index("tm") == blocks * STEPS - 1, 0.0, 1.0).astype(F32)
    for comp in (0, 1):
        for i in range(4):
            mid[comp, pl.ds(i * LANE, LANE), :] = turned(back_rows, i, comp) * live
    first.stage(0)
    for block in range(4):
        begin = block // 2 * 2 * LANE + block % 2
        for comp in (0, 1):
            rows = mid[comp, pl.ds(begin, LANE, stride=2), :]
            back[pl.ds(block * LANE, LANE), pl.ds(comp * LANE, LANE)] = rows
    first.stage(1)

    @pl.when(place.z == 0)
    def _():
        row = lax.broadcasted_iota(jnp.int32, (PAD, LANE), 0)
        lane = lax.broadcasted_iota(jnp.int32, (PAD, LANE), 1)
        for block in range(4):
            total = jnp.zeros((PAD, LANE), F32)
            for i in range(paths // LANE):
                wanted = lane + i * LANE == row + (place.q * 2 + core) * share
                pick = jnp.where(jnp.logical_and(wanted, row < share), 1.0, 0.0).astype(BF16)
                rest = start_rows[i, pl.ds(block // 2 * 2 * LANE + block % 2, LANE, stride=2), :]
                for _ in range(3):
                    part = rest.astype(BF16)
                    rest = rest - part.astype(F32)
                    total += lax.dot_general(pick, part, (((1,), (1,)), ((), ())), preferred_element_type=F32)
            prior[:, block * LANE:(block + 1) * LANE] = total

    @pl.when(place.z > 0)
    def _():
        prior[...] = jnp.zeros_like(prior)

    decay = jnp.exp(-rates[...])
    own = (decay * (1.0 + rates[...]), decay * (1.0 - rates[...]))
    other = (decay, -decay * rates[...] * rates[...])

    def ordered(pair):
        return jnp.concatenate([pair[comp][:, half * LANE:(half + 1) * LANE] for half in (0, 1) for comp in (0, 1)], 1)

    alpha, beta = ordered(own), ordered(other)
    first.stage(2)
    first.stage(3)
    second.begin()
    first.finish()
    for copy in watch:
        copy.wait()
    own_obs.wait()

    def moved(state):
        swap = jnp.concatenate([state[:, i * LANE:(i + 1) * LANE] for i in (1, 0, 3, 2)], 1)
        return alpha * state + beta * swap

    def values(state):
        return jnp.concatenate([state[:, :LANE], state[:, 2 * LANE:3 * LANE]], 1)

    row = lax.broadcasted_iota(jnp.int32, (PAD, 4 * LANE), 0)
    lane = lax.broadcasted_iota(jnp.int32, (PAD, 4 * LANE), 1)
    unit = jnp.where(lane == row + (place.q * 2 + core) * PAD, 1.0, 0.0).astype(F32)
    zero = jnp.zeros((PAD, 4 * LANE), F32)
    last = blocks - 1

    def forward(k, state):
        predicted = moved(state)
        target, rows = seen[k], state.shape[0]
        if rows > PAD:
            target = jnp.concatenate([target, jnp.zeros((rows - PAD, 2 * LANE), F32)], 0)
        innovation = target - values(predicted)
        state = predicted + jnp.concatenate([product(innovation, gains[k, half]) for half in (0, 1)], 1)
        kept[k] = state[:PAD]
        return state

    def mapped(state, table):
        return product(state, table[...].reshape(4 * LANE, 4 * LANE))

    both = lax.fori_loop(0, STEPS, forward, jnp.concatenate([prior[...], unit], 0))
    leave[...] = both[:PAD]
    stage[...] = both[PAD:]
    up = remote(leave, enter, chain.at[0], chain.at[1], place.above(1))
    maps = GatherRows(place, stage, pmap, msend.at[0], mrecv.at[0], mside_s.at[0], mside_r.at[0], local.at[3])
    through = jnp.logical_and(place.z >= 2, place.z < last)

    @pl.when(place.z == 0)
    def _():
        up.start()

    @pl.when(through)
    def _():
        maps.begin()

    second.stage(0)

    def filter_again():
        return lax.fori_loop(0, STEPS, forward, enter[...])

    @pl.when(place.z == 1)
    def _():
        up.wait_recv()
        leave[...] = filter_again()
        up.start()

    @pl.when(through)
    def _():
        maps.finish()
    second.stage(1)

    @pl.when(place.z >= last - 1)
    def _():
        second.stage(2)

    @pl.when(place.z >= 2)
    def _():
        up.wait_recv()

    @pl.when(through)
    def _():
        leave[...] = leave[...] + mapped(enter[...], pmap)
        up.start()

    @pl.when(place.z < last - 1)
    def _():
        second.stage(2)

    second.stage(3)

    @pl.when(place.z >= 2)
    def _():
        filter_again()

    @pl.when(place.z < last)
    def _():
        up.wait_send()
    second.finish()

    def back_product(k, value):
        return jnp.concatenate([product(value, backs[k, half]) for half in (0, 1)], 1)

    def keep_smooth(k, state):
        sout[k, 0] = state[:, :2 * LANE]
        sout[k, 1] = state[:, 2 * LANE:]

    def both_back(i, state):
        k = STEPS - 1 - i
        held = kept[k]
        wanted = jnp.concatenate([state[:PAD] - moved(held), state[PAD:]], 0)
        state = jnp.concatenate([held, zero], 0) + back_product(k, wanted)
        keep_smooth(k, state[:PAD])
        return state

    both = lax.fori_loop(0, STEPS, both_back, jnp.concatenate([zero, unit], 0))
    turn[...] = both[PAD:]
    far[0] = both[:PAD]
    turns = GatherRows(place, turn, qmap, msend.at[1], mrecv.at[1], mside_s.at[1], mside_r.at[1], local.at[4])
    down = remote(far.at[0], far.at[1], chain.at[2], chain.at[3], place.above(-1))
    through = jnp.logical_and(place.z >= 1, place.z < last - 1)

    def hand_on(value_ref, k, out, sem):
        for half in (0, 1):
            part = value_ref.at[k, half]
            home = jnp.logical_and(k == place.q, core == half)

            @pl.when(home)
            def _():
                pltpu.make_async_copy(part, out.at[place.q, core], sem.at[1]).start()

            @pl.when(jnp.logical_not(home))
            def _():
                remote(part, out.at[place.q, core], sem.at[0], sem.at[1], place.device(k, half)).start()

    def hand_filtered(k, carry):
        fsend[k, 0] = kept[k, :, pl.ds(0, 2 * LANE)]
        fsend[k, 1] = kept[k, :, pl.ds(2 * LANE, 2 * LANE)]
        hand_on(fsend, k, filt, fsem)
        return carry

    def hand_smoothed(i, carry):
        hand_on(sout, STEPS - 1 - i, smooth, ssem)
        return carry

    def all_handed(out, sem):
        pltpu.make_async_copy(out, out, sem.at[1]).wait()
        rest = out.at[pl.ds(0, STEPS - 1)]
        pltpu.make_async_copy(rest, rest, sem.at[0]).wait()
        pltpu.make_async_copy(out.at[0, 0], out.at[0, 0], sem.at[0]).wait()

    def emit(table, rows):
        for i in range(2 * STEPS):
            spread[pl.ds(i * share, share), :] = table[i // 2, i % 2, pl.ds(0, share), :]
        for comp in (0, 1):
            for i in range(paths // LANE):
                block = spread[pl.ds(i * LANE, LANE), pl.ds(comp * LANE, LANE)]
                woven[i, pl.ds(comp, LANE, stride=2), :] = block.T
        for i in range(paths // LANE):
            rows[:, i * LANE:(i + 1) * LANE] = woven[i]

    def smooth_again():
        def step(i, state):
            k = STEPS - 1 - i
            state = kept[k] + back_product(k, state - moved(kept[k]))
            keep_smooth(k, state)
            hand_on(sout, k, smooth, ssem)
            return state

        return lax.fori_loop(0, STEPS, step, far[1])

    @pl.when(place.z == last)
    def _():
        down.start()

    @pl.when(through)
    def _():
        turns.begin()

    @pl.when(place.z == last - 1)
    def _():
        down.wait_recv()
        far[0] = smooth_again()
        down.start()

    @pl.when(through)
    def _():
        turns.finish()
    lax.fori_loop(0, STEPS, hand_filtered, 0)

    @pl.when(place.z == last)
    def _():
        lax.fori_loop(0, STEPS, hand_smoothed, 0)

    @pl.when(place.z < last // 2)
    def _():
        all_handed(filt, fsem)
        emit(filt, filt_rows)

    @pl.when(place.z < last - 1)
    def _():
        down.wait_recv()

    @pl.when(through)
    def _():
        far[0] = far[0] + mapped(far[1], qmap)
        down.start()

    @pl.when(place.z < last - 1)
    def _():
        smooth_again()

    @pl.when(place.z > 0)
    def _():
        down.wait_send()

    @pl.when(place.z >= last // 2)
    def _():
        all_handed(filt, fsem)
        emit(filt, filt_rows)

    all_handed(smooth, ssem)
    emit(smooth, smooth_rows)


def body(site_rates, prior_mean, observed, obs_mask, filter_gains, smooth_gains):
    blocks = lax.axis_size("tm") // STEPS
    paths = prior_mean.shape[1]
    vmem, dma = pl.BlockSpec(memory_space=pltpu.VMEM), pltpu.SemaphoreType.DMA
    out = jax.ShapeDtypeStruct((2 * LANE, paths), F32)
    shared = (STEPS, 2, PAD, 2 * LANE)
    wide = (STEPS, 2, PAD, 4 * LANE)
    narrow = (PAD, 4 * LANE)
    sizes = [
        (2 * LANE, 2 * LANE), (4 * LANE, 2 * LANE), (2, 4 * LANE, LANE), (4, 2 * LANE, LANE),
        (paths // LANE, 4 * LANE, LANE), (paths // LANE, 2 * LANE, LANE), (paths, 2 * LANE), shared, narrow, shared, shared,
        (STEPS, 2, 2 * LANE, 2 * LANE), (STEPS, 2, 4 * LANE, 2 * LANE), (STEPS, PAD, 2 * LANE), (STEPS, PAD, 4 * LANE),
        wide, wide, narrow, narrow, narrow, narrow, (2, *narrow), shared, shared,
    ]
    filt, smooth = pl.pallas_call(
        functools.partial(kernel, blocks),
        out_shape=(out, out),
        in_specs=[vmem] * 4 + [pl.BlockSpec(memory_space=pl.ANY)] * 2,
        out_specs=(vmem, vmem),
        scratch_shapes=[pltpu.VMEM(size, F32) for size in sizes] + [
            dma((40,)), dma((40,)), dma((32,)), dma((32,)),
            dma((40,)), dma((40,)), dma((32,)), dma((32,)),
            dma((STEPS,)), dma((STEPS,)),
            dma((2, STEPS)), dma((2, STEPS)), dma((2, STEPS)), dma((2, STEPS)),
            dma((4,)), dma((2,)), dma((2,)), dma((12,)),
        ],
        compiler_params=pltpu.CompilerParams(
            collective_id=0, has_side_effects=True, vmem_limit_bytes=60 * 1024 * 1024
        ),
        name="two_level_scan",
    )(site_rates[None], obs_mask, filter_gains[0], observed[0], smooth_gains[0], prior_mean)
    return filt[None], smooth[None]


def solution(mesh):
    placed = (
        P(),
        P(),
        P("tm", None, None),
        P("tm", None),
        P("tm", "rows", None),
        P("tm", "rows", None),
    )
    return jax.shard_map(
        body,
        mesh=mesh,
        in_specs=placed,
        out_specs=(P("tm", "rows", None), P("tm", "rows", None)),
        check_vma=False,
    )
```

```python
import functools

import jax
import jax.numpy as jnp
from jax import lax
from jax.experimental import pallas as pl
from jax.experimental.pallas import tpu as pltpu
from jax.sharding import PartitionSpec as P

F32, BF16 = jnp.float32, jnp.bfloat16
SIDE = 4
STEPS = SIDE * SIDE
LANE = 128
PAD = 16


def halves(value):
    high = value.astype(BF16)
    return high, (value - high.astype(F32)).astype(BF16)


def product(left, right):
    dot = functools.partial(jnp.dot, preferred_element_type=F32)
    left_high, left_low = halves(left)
    right_high, right_low = halves(right)
    rows = left.shape[0]
    both = dot(jnp.concatenate([left_high, left_low], 0), right_high)
    return both[:rows] + (both[rows:] + dot(left_high, right_low))


class Place:
    def __init__(self, blocks):
        time = lax.axis_index("tm")
        self.blocks = blocks
        self.z, self.q = lax.div(time, STEPS), lax.rem(time, STEPS)
        self.y, self.x = lax.div(self.q, SIDE), lax.rem(self.q, SIDE)
        self.core = lax.axis_index("rows")
        self.partner = {"tm": time, "rows": 1 - self.core}

    def chip(self, dy, dx):
        return lax.rem(self.y + dy % SIDE, SIDE) * SIDE + lax.rem(self.x + dx % SIDE, SIDE)

    def device(self, q, core):
        return {"tm": self.z * STEPS + q, "rows": core}

    def above(self, dz):
        z = lax.rem(self.z + dz % self.blocks, self.blocks)
        return {"tm": z * STEPS + self.q, "rows": self.core}


def remote(src, dst, send, recv, device):
    return pltpu.make_async_remote_copy(
        src_ref=src, dst_ref=dst, send_sem=send, recv_sem=recv, device_id=device, device_id_type=pl.DeviceIdType.MESH
    )


class Gather:
    def __init__(self, place, own, buf, send, recv, side_send, side_recv, local):
        self.place, self.own, self.buf = place, own, buf
        self.half, self.quarter = own.shape[0] // 2, own.shape[0] // 4
        self.sems, self.side_sems = (send, recv), (side_send, side_recv)
        self.keep = pltpu.make_async_copy(own, buf.at[place.q, place.core], local)
        signs, sides = (1, -1), (0, 1)
        keys = [("a1", h, s) for h in sides for s in signs] + [("a2", h, s) for h in sides for s in signs]
        keys += [(name, h, o, s) for name in ("b1", "b2") for h in sides for o in (0, -1, 1, 2) for s in signs]
        self.keys = {key: i for i, key in enumerate(keys)}

    @staticmethod
    def off(h, along, across=0):
        return ((across, along), (along, across))[h]

    def copy(self, key):
        name, h, s = key[0], key[1], key[-1]
        start, size = h * self.half, self.half
        if name == "a1":
            offset, to = (0, 0), self.off(h, s)
        elif name == "a2":
            offset, to = self.off(h, -s), self.off(h, s)
        elif name == "b1":
            offset, to = self.off(h, key[2]), self.off(h, 0, s)
        else:
            offset, to = self.off(h, key[2], -s), self.off(h, 0, s)
        if name in ("a2", "b2"):
            start, size = start + (self.quarter if s < 0 else 0), self.quarter
        place, i = self.place, self.keys[key]
        dst = self.buf.at[place.chip(*offset), place.core, pl.ds(start, size)]
        src = self.own.at[pl.ds(start, size)] if offset == (0, 0) else dst
        return remote(src, dst, self.sems[0].at[i], self.sems[1].at[i], place.device(place.chip(*to), place.core))

    def across(self, h, offset):
        place, dy, dx = self.place, offset[0] % SIDE, offset[1] % SIDE
        i = h * STEPS + dy * SIDE + dx
        part = pl.ds(h * self.half, self.half)
        dst = self.buf.at[place.chip(dy, dx), place.core, part]
        src = self.own.at[part] if (dy, dx) == (0, 0) else dst
        return remote(src, dst, self.side_sems[0].at[i], self.side_sems[1].at[i], place.partner)

    def begin(self):
        for name, rest in (("a1", ()), ("b1", (0,))):
            for h in (0, 1):
                for s in (1, -1):
                    self.copy((name, h, *rest, s)).start()
        for h in (0, 1):
            self.across(h, (0, 0)).start()
        self.keep.start()

    def relay(self, h, o, s):
        self.copy(("b1", h, o, s)).wait_recv()
        self.copy(("b2", h, o, s)).start()
        self.across(h, self.off(h, o, -s)).start()

    def stage(self, number):
        if number == 0:
            for s in (1, -1):
                for h in (0, 1):
                    self.copy(("a1", h, s)).wait_recv()
                    self.copy(("a2", h, s)).start()
                    for t in (1, -1):
                        self.copy(("b1", h, -s, t)).start()
                    self.across(h, self.off(h, -s)).start()
        if number == 1:
            for s in (1, -1):
                for h in (0, 1):
                    self.relay(h, 0, s)
            for h in (0, 1):
                for s in (1, -1):
                    self.copy(("a2", h, s)).wait_recv()
                for t in (1, -1):
                    self.copy(("b1", h, 2, t)).start()
                self.across(h, self.off(h, 2)).start()
        if number in (2, 3):
            for o in ((-1, 1), (2,))[number - 2]:
                for s in (1, -1):
                    for h in (0, 1):
                        self.relay(h, o, s)

    def finish(self):
        for o in (0, -1, 1, 2):
            for h in (0, 1):
                for s in (1, -1):
                    self.copy(("b2", h, o, s)).wait_recv()
                self.across(h, self.off(h, o, 2)).start()
        for i in range(STEPS):
            for h in (0, 1):
                self.across(h, divmod(i, SIDE)).wait_recv()
        self.keep.wait()

    def drain(self):
        for i in range(STEPS):
            for h in (0, 1):
                self.across(h, divmod(i, SIDE)).wait_send()
        for key in self.keys:
            self.copy(key).wait_send()


class GatherRows:
    def __init__(self, place, own, buf, send, recv, side_send, side_recv, local):
        self.place, self.own, self.buf = place, own, buf
        self.sems, self.side_sems = (send, recv), (side_send, side_recv)
        self.keep = pltpu.make_async_copy(own, buf.at[place.q, place.core], local)
        self.order = sorted(range(1, STEPS), key=lambda i: -sum(min(k, SIDE - k) for k in divmod(i, SIDE)))

    def copy(self, i):
        place, (dy, dx) = self.place, divmod(i, SIDE)
        to = place.device(place.chip(dy, dx), place.core)
        return remote(self.own, self.buf.at[place.q, place.core], self.sems[0].at[i], self.sems[1].at[i], to)

    def across(self, i):
        place, (dy, dx) = self.place, divmod(i, SIDE)
        dst = self.buf.at[place.chip(-dy, -dx), place.core]
        return remote(dst if i else self.own, dst, self.side_sems[0].at[i], self.side_sems[1].at[i], place.partner)

    def begin(self):
        for i in self.order:
            self.copy(i).start()
        self.across(0).start()
        self.keep.start()

    def finish(self):
        for i in reversed(self.order):
            self.copy(i).wait_recv()
            self.across(i).start()
        for i in range(STEPS):
            self.across(i).wait_recv()
        self.keep.wait()

    def drain(self):
        for i in range(STEPS):
            self.across(i).wait_send()
        for i in self.order:
            self.copy(i).wait_send()


def turned(ref, i, start):
    return ref[i, pl.ds(start, LANE, stride=2), :].T


def kernel(blocks, rates, mask, gain_rows, watched, back_hbm, start_hbm, filt_rows, smooth_rows,
           gain, back, mid, back_rows, start_rows, woven, spread, obs, prior, filt, smooth,
           gains, backs, seen, kept, pmap, qmap, parts, stage, enter, leave, turn, far, near, sout, fsend,
           ksend, krecv, kside_s, kside_r, gsend, grecv, gside_s, gside_r,
           osend, orecv, msend, mrecv, mside_s, mside_r, chain, fsem, ssem, local):
    place = Place(blocks)
    core = place.core
    share = watched.shape[1] // (2 * STEPS)
    paths = watched.shape[1]
    barrier = pltpu.get_barrier_semaphore()
    greet = [place.partner, place.above(1), place.above(-1)]
    for i in range(1, STEPS):
        q = place.chip(*divmod(i, SIDE))
        greet += [place.device(q, core), place.device(q, 1 - core)]
    for device in greet:
        pl.semaphore_signal(barrier, inc=1, device_id=device, device_id_type=pl.DeviceIdType.MESH)
    loads = []
    for i in range(4):
        loads.append(pltpu.make_async_copy(back_hbm.at[:, pl.ds(i * LANE, LANE)], back_rows.at[i], local.at[5 + i]))
    for i in range(paths // LANE):
        loads.append(pltpu.make_async_copy(start_hbm.at[:, pl.ds(i * LANE, LANE)], start_rows.at[i], local.at[9 + i]))
    for load in loads:
        load.start()

    kept_gain = gain_rows[...] * mask[...].astype(F32)
    for i in (0, 1):
        mid[i, pl.ds(0, 2 * LANE), :] = kept_gain[:, i * LANE:(i + 1) * LANE]
        for comp in (0, 1):
            gain[i * LANE:(i + 1) * LANE, comp * LANE:(comp + 1) * LANE] = turned(mid, i, comp)
    pl.semaphore_wait(barrier, len(greet))
    first = Gather(place, gain, gains, ksend, krecv, kside_s, kside_r, local.at[1])
    second = Gather(place, back, backs, gsend, grecv, gside_s, gside_r, local.at[2])
    first.begin()

    for load in loads:
        load.wait()
    live = jnp.where(lax.axis_index("tm") == blocks * STEPS - 1, 0.0, 1.0).astype(F32)
    for comp in (0, 1):
        for i in range(4):
            mid[comp, pl.ds(i * LANE, LANE), :] = turned(back_rows, i, comp) * live
    first.stage(0)
    for block in range(4):
        begin = block // 2 * 2 * LANE + block % 2
        for comp in (0, 1):
            rows = mid[comp, pl.ds(begin, LANE, stride=2), :]
            back[pl.ds(block * LANE, LANE), pl.ds(comp * LANE, LANE)] = rows
    first.stage(1)

    sites = watched[...].T
    for i in range(2 * STEPS):
        obs[i // 2, i % 2] = sites[i * share:(i + 1) * share]
    watch = []
    for i in range(1, STEPS):
        q = place.chip(*divmod(i, SIDE))
        copy = remote(obs.at[q, core], seen.at[place.q], osend.at[i], orecv.at[i], place.device(q, core))
        copy.start()
        watch.append(copy)
    own_obs = pltpu.make_async_copy(obs.at[place.q, core], seen.at[place.q], local.at[0])
    own_obs.start()

    @pl.when(place.z == 0)
    def _():
        row = lax.broadcasted_iota(jnp.int32, (PAD, LANE), 0)
        lane = lax.broadcasted_iota(jnp.int32, (PAD, LANE), 1)
        for block in range(4):
            total = jnp.zeros((PAD, LANE), F32)
            for i in range(paths // LANE):
                wanted = lane + i * LANE == row + (place.q * 2 + core) * share
                pick = jnp.where(jnp.logical_and(wanted, row < share), 1.0, 0.0).astype(BF16)
                rest = start_rows[i, pl.ds(block // 2 * 2 * LANE + block % 2, LANE, stride=2), :]
                for _ in range(3):
                    part = rest.astype(BF16)
                    rest = rest - part.astype(F32)
                    total += lax.dot_general(pick, part, (((1,), (1,)), ((), ())), preferred_element_type=F32)
            prior[:, block * LANE:(block + 1) * LANE] = total

    @pl.when(place.z > 0)
    def _():
        prior[...] = jnp.zeros_like(prior)

    decay = jnp.exp(-rates[...])
    own = (decay * (1.0 + rates[...]), decay * (1.0 - rates[...]))
    other = (decay, -decay * rates[...] * rates[...])

    def ordered(pair):
        return jnp.concatenate([pair[comp][:, half * LANE:(half + 1) * LANE] for half in (0, 1) for comp in (0, 1)], 1)

    alpha, beta = ordered(own), ordered(other)
    first.stage(2)
    first.stage(3)
    second.begin()
    first.finish()
    for copy in watch:
        copy.wait_recv()
    own_obs.wait()

    def moved(state):
        swap = jnp.concatenate([state[:, i * LANE:(i + 1) * LANE] for i in (1, 0, 3, 2)], 1)
        return alpha * state + beta * swap

    def values(state):
        return jnp.concatenate([state[:, :LANE], state[:, 2 * LANE:3 * LANE]], 1)

    row = lax.broadcasted_iota(jnp.int32, (PAD, 4 * LANE), 0)
    lane = lax.broadcasted_iota(jnp.int32, (PAD, 4 * LANE), 1)
    unit = jnp.where(lane == row + (place.q * 2 + core) * PAD, 1.0, 0.0).astype(F32)
    zero = jnp.zeros((PAD, 4 * LANE), F32)
    last = blocks - 1

    def forward(k, state):
        predicted = moved(state)
        target = jnp.concatenate([seen[k], jnp.zeros((state.shape[0] - share, 2 * LANE), F32)], 0)
        innovation = target - values(predicted)
        state = predicted + jnp.concatenate([product(innovation, gains[k, half]) for half in (0, 1)], 1)
        kept[k] = state[:PAD]
        return state

    def whole(ref):
        state = jnp.concatenate([ref[0], ref[1]], 1)
        return jnp.concatenate([state, jnp.zeros((PAD - share, 4 * LANE), F32)], 0)

    def put(ref, state):
        for half in (0, 1):
            ref[half] = state[:share, half * 2 * LANE:(half + 1) * 2 * LANE]

    def parts_of(table):
        for q in range(STEPS):
            for i in (0, 1):
                high, low = halves(table[q, i])
                rows = pl.ds((q * 2 + i) * PAD, PAD)
                parts[0, rows, :] = high
                parts[1, rows, :] = low

    def hop(link, given, offset):
        dot = functools.partial(jnp.dot, preferred_element_type=F32)
        pair = []
        for half in (0, 1):
            link[half].wait_recv()
            value = jnp.concatenate([given[half], jnp.zeros((PAD - share, 2 * LANE), F32)], 0)
            high, low = halves(value)
            pair.append((high, jnp.concatenate([high, low], 0)))
        for half in (0, 1):
            lanes = pl.ds(half * 2 * LANE, 2 * LANE)
            total = offset[half]
            for part in (0, 1):
                rows = pl.ds(part * 2 * LANE, 2 * LANE)
                both = dot(pair[part][1], parts[0, rows, lanes])
                total += (both[:PAD] + (both[PAD:] + dot(pair[part][0], parts[1, rows, lanes])))[:share]
            offset[half] = total
            link[half].start()

    both = lax.fori_loop(0, STEPS, forward, jnp.concatenate([prior[...], unit], 0))
    put(leave, both)
    stage[...] = both[PAD:]
    up = [remote(leave.at[i], enter.at[i], chain.at[0, i], chain.at[1, i], place.above(1)) for i in (0, 1)]
    maps = GatherRows(place, stage, pmap, msend.at[0], mrecv.at[0], mside_s.at[0], mside_r.at[0], local.at[3])
    through = jnp.logical_and(place.z >= 2, place.z < last)

    @pl.when(place.z == 0)
    def _():
        for copy in up:
            copy.start()

    @pl.when(through)
    def _():
        maps.begin()

    second.stage(0)

    def filter_again():
        return lax.fori_loop(0, STEPS, forward, whole(enter))

    @pl.when(place.z == 1)
    def _():
        for copy in up:
            copy.wait_recv()
        put(leave, filter_again())
        for copy in up:
            copy.start()

    @pl.when(through)
    def _():
        maps.finish()
        parts_of(pmap)
    second.stage(1)

    @pl.when(place.z >= last - 1)
    def _():
        second.stage(2)

    @pl.when(place.z == last)
    def _():
        for copy in up:
            copy.wait_recv()

    @pl.when(through)
    def _():
        hop(up, enter, leave)

    @pl.when(place.z < last - 1)
    def _():
        second.stage(2)

    second.stage(3)

    @pl.when(place.z >= 2)
    def _():
        filter_again()

    second.finish()

    def back_product(k, value):
        return jnp.concatenate([product(value, backs[k, half]) for half in (0, 1)], 1)

    def keep_smooth(k, state):
        put(sout.at[k], state)

    def both_back(i, state):
        k = STEPS - 1 - i
        held = kept[k]
        wanted = jnp.concatenate([state[:PAD] - moved(held), state[PAD:]], 0)
        state = jnp.concatenate([held, zero], 0) + back_product(k, wanted)
        keep_smooth(k, state[:PAD])
        return state

    both = lax.fori_loop(0, STEPS, both_back, jnp.concatenate([zero, unit], 0))
    turn[...] = both[PAD:]
    put(far, both)
    turns = GatherRows(place, turn, qmap, msend.at[1], mrecv.at[1], mside_s.at[1], mside_r.at[1], local.at[4])
    down = [remote(far.at[i], near.at[i], chain.at[2, i], chain.at[3, i], place.above(-1)) for i in (0, 1)]
    through = jnp.logical_and(place.z >= 1, place.z < last - 1)

    def hand_on(value_ref, k, out, sem):
        for half in (0, 1):
            part = value_ref.at[k, half]
            home = jnp.logical_and(k == place.q, core == half)

            @pl.when(home)
            def _():
                pltpu.make_async_copy(part, out.at[place.q, core], sem.at[1]).start()

            @pl.when(jnp.logical_not(home))
            def _():
                remote(part, out.at[place.q, core], sem.at[0], sem.at[1], place.device(k, half)).start()

    def hand_filtered(k, carry):
        put(fsend.at[k], kept[k])
        hand_on(fsend, k, filt, fsem)
        return carry

    def hand_smoothed(i, carry):
        hand_on(sout, STEPS - 1 - i, smooth, ssem)
        return carry

    def all_handed(out, sem):
        pltpu.make_async_copy(out, out, sem.at[1]).wait()
        rest = out.at[pl.ds(0, STEPS - 1)]
        pltpu.make_async_copy(rest, rest, sem.at[0]).wait()
        pltpu.make_async_copy(out.at[0, 0], out.at[0, 0], sem.at[0]).wait()

    def emit(table, rows):
        for i in range(2 * STEPS):
            spread[pl.ds(i * share, share), :] = table[i // 2, i % 2]
        for comp in (0, 1):
            for i in range(paths // LANE):
                block = spread[pl.ds(i * LANE, LANE), pl.ds(comp * LANE, LANE)]
                woven[i, pl.ds(comp, LANE, stride=2), :] = block.T
        for i in range(paths // LANE):
            rows[:, i * LANE:(i + 1) * LANE] = woven[i]

    def smooth_again():
        def step(i, state):
            k = STEPS - 1 - i
            state = kept[k] + back_product(k, state - moved(kept[k]))
            keep_smooth(k, state)
            hand_on(sout, k, smooth, ssem)
            return state

        return lax.fori_loop(0, STEPS, step, whole(near))

    @pl.when(place.z == last)
    def _():
        for copy in down:
            copy.start()

    @pl.when(through)
    def _():
        turns.begin()

    @pl.when(place.z == last - 1)
    def _():
        for copy in down:
            copy.wait_recv()
        put(far, smooth_again())
        for copy in down:
            copy.start()

    @pl.when(through)
    def _():
        turns.finish()
        parts_of(qmap)

    def hand_all_filtered():
        lax.fori_loop(0, STEPS, hand_filtered, 0)

    early = place.z < last // 2 + 1

    @pl.when(early)
    def _():
        hand_all_filtered()

    @pl.when(place.z < last // 2)
    def _():
        all_handed(filt, fsem)
        emit(filt, filt_rows)

    @pl.when(place.z == 0)
    def _():
        for copy in down:
            copy.wait_recv()

    @pl.when(through)
    def _():
        hop(down, near, far)

    @pl.when(jnp.logical_not(early))
    def _():
        hand_all_filtered()

    @pl.when(place.z == last)
    def _():
        lax.fori_loop(0, STEPS, hand_smoothed, 0)

    @pl.when(place.z < last - 1)
    def _():
        smooth_again()

    @pl.when(place.z >= last // 2)
    def _():
        all_handed(filt, fsem)
        emit(filt, filt_rows)

    @pl.when(place.z < last)
    def _():
        for copy in up:
            copy.wait_send()

    @pl.when(place.z > 0)
    def _():
        for copy in down:
            copy.wait_send()

    @pl.when(jnp.logical_and(place.z >= 2, place.z < last))
    def _():
        maps.drain()

    @pl.when(through)
    def _():
        turns.drain()

    first.drain()
    second.drain()
    for copy in watch:
        copy.wait_send()
    all_handed(smooth, ssem)
    emit(smooth, smooth_rows)


def body(site_rates, prior_mean, observed, obs_mask, filter_gains, smooth_gains):
    blocks = lax.axis_size("tm") // STEPS
    paths = prior_mean.shape[1]
    vmem, dma = pl.BlockSpec(memory_space=pltpu.VMEM), pltpu.SemaphoreType.DMA
    out = jax.ShapeDtypeStruct((2 * LANE, paths), F32)
    share = paths // (2 * STEPS)
    shared, chained = (STEPS, 2, share, 2 * LANE), (2, share, 2 * LANE)
    wide = (STEPS, 2, PAD, 4 * LANE)
    narrow = (PAD, 4 * LANE)
    sizes = [
        (2 * LANE, 2 * LANE), (4 * LANE, 2 * LANE), (2, 4 * LANE, LANE), (4, 2 * LANE, LANE),
        (paths // LANE, 4 * LANE, LANE), (paths // LANE, 2 * LANE, LANE), (paths, 2 * LANE), shared, narrow, shared, shared,
        (STEPS, 2, 2 * LANE, 2 * LANE), (STEPS, 2, 4 * LANE, 2 * LANE), (STEPS, share, 2 * LANE), (STEPS, PAD, 4 * LANE),
        wide, wide, (BF16, 2, 4 * LANE, 4 * LANE), narrow, chained, chained, narrow, chained, chained, shared, shared,
    ]
    filt, smooth = pl.pallas_call(
        functools.partial(kernel, blocks),
        out_shape=(out, out),
        in_specs=[vmem] * 4 + [pl.BlockSpec(memory_space=pl.ANY)] * 2,
        out_specs=(vmem, vmem),
        scratch_shapes=[pltpu.VMEM(size[-3:], BF16) if size[0] is BF16 else pltpu.VMEM(size, F32) for size in sizes] + [
            dma((40,)), dma((40,)), dma((32,)), dma((32,)),
            dma((40,)), dma((40,)), dma((32,)), dma((32,)),
            dma((STEPS,)), dma((STEPS,)),
            dma((2, STEPS)), dma((2, STEPS)), dma((2, STEPS)), dma((2, STEPS)),
            dma((4, 2)), dma((2,)), dma((2,)), dma((12,)),
        ],
        compiler_params=pltpu.CompilerParams(
            collective_id=0, has_side_effects=True, vmem_limit_bytes=60 * 1024 * 1024
        ),
        name="two_level_scan",
    )(site_rates[None], obs_mask, filter_gains[0], observed[0], smooth_gains[0], prior_mean)
    return filt[None], smooth[None]


def solution(mesh):
    placed = (
        P(),
        P(),
        P("tm", None, None),
        P("tm", None),
        P("tm", "rows", None),
        P("tm", "rows", None),
    )
    return jax.shard_map(
        body,
        mesh=mesh,
        in_specs=placed,
        out_specs=(P("tm", "rows", None), P("tm", "rows", None)),
        check_vma=False,
    )
```

```python
import functools

import jax
import jax.numpy as jnp
from jax import lax
from jax.experimental import pallas as pl
from jax.experimental.pallas import tpu as pltpu
from jax.sharding import PartitionSpec as P

F32, BF16 = jnp.float32, jnp.bfloat16
SIDE = 4
STEPS = SIDE * SIDE
LANE = 128
DIRECT = 5
PAD = 16


def halves(value):
    high = value.astype(BF16)
    return high, (value - high.astype(F32)).astype(BF16)


def product(left, right):
    dot = functools.partial(jnp.dot, preferred_element_type=F32)
    left_high, left_low = halves(left)
    right_high, right_low = halves(right)
    rows = left.shape[0]
    both = dot(jnp.concatenate([left_high, left_low], 0), right_high)
    return both[:rows] + (both[rows:] + dot(left_high, right_low))


class Place:
    def __init__(self, blocks):
        time = lax.axis_index("tm")
        self.blocks = blocks
        self.z, self.q = lax.div(time, STEPS), lax.rem(time, STEPS)
        self.y, self.x = lax.div(self.q, SIDE), lax.rem(self.q, SIDE)
        self.core = lax.axis_index("rows")
        self.partner = {"tm": time, "rows": 1 - self.core}

    def chip(self, dy, dx):
        return lax.rem(self.y + dy % SIDE, SIDE) * SIDE + lax.rem(self.x + dx % SIDE, SIDE)

    def device(self, q, core):
        return {"tm": self.z * STEPS + q, "rows": core}

    def above(self, dz):
        z = lax.rem(self.z + dz % self.blocks, self.blocks)
        return {"tm": z * STEPS + self.q, "rows": self.core}


def remote(src, dst, send, recv, device):
    return pltpu.make_async_remote_copy(
        src_ref=src, dst_ref=dst, send_sem=send, recv_sem=recv, device_id=device, device_id_type=pl.DeviceIdType.MESH
    )


class Gather:
    def __init__(self, place, own, buf, send, recv, side_send, side_recv, local):
        self.place, self.own, self.buf = place, own, buf
        self.half, self.quarter = own.shape[0] // 2, own.shape[0] // 4
        self.sems, self.side_sems = (send, recv), (side_send, side_recv)
        self.keep = pltpu.make_async_copy(own, buf.at[place.q, place.core], local)
        signs, sides = (1, -1), (0, 1)
        keys = [("a1", h, s) for h in sides for s in signs] + [("a2", h, s) for h in sides for s in signs]
        keys += [(name, h, o, s) for name in ("b1", "b2") for h in sides for o in (0, -1, 1, 2) for s in signs]
        self.keys = {key: i for i, key in enumerate(keys)}

    @staticmethod
    def off(h, along, across=0):
        return ((across, along), (along, across))[h]

    def copy(self, key):
        name, h, s = key[0], key[1], key[-1]
        start, size = h * self.half, self.half
        if name == "a1":
            offset, to = (0, 0), self.off(h, s)
        elif name == "a2":
            offset, to = self.off(h, -s), self.off(h, s)
        elif name == "b1":
            offset, to = self.off(h, key[2]), self.off(h, 0, s)
        else:
            offset, to = self.off(h, key[2], -s), self.off(h, 0, s)
        if name in ("a2", "b2"):
            start, size = start + (self.quarter if s < 0 else 0), self.quarter
        place, i = self.place, self.keys[key]
        dst = self.buf.at[place.chip(*offset), place.core, pl.ds(start, size)]
        src = self.own.at[pl.ds(start, size)] if offset == (0, 0) else dst
        return remote(src, dst, self.sems[0].at[i], self.sems[1].at[i], place.device(place.chip(*to), place.core))

    def across(self, h, offset):
        place, dy, dx = self.place, offset[0] % SIDE, offset[1] % SIDE
        i = h * STEPS + dy * SIDE + dx
        part = pl.ds(h * self.half, self.half)
        dst = self.buf.at[place.chip(dy, dx), place.core, part]
        src = self.own.at[part] if (dy, dx) == (0, 0) else dst
        return remote(src, dst, self.side_sems[0].at[i], self.side_sems[1].at[i], place.partner)

    def begin(self):
        for name, rest in (("a1", ()), ("b1", (0,))):
            for h in (0, 1):
                for s in (1, -1):
                    self.copy((name, h, *rest, s)).start()
        for h in (0, 1):
            self.across(h, (0, 0)).start()
        self.keep.start()

    def relay(self, h, o, s):
        self.copy(("b1", h, o, s)).wait_recv()
        self.copy(("b2", h, o, s)).start()
        self.across(h, self.off(h, o, -s)).start()

    def stage(self, number):
        if number == 0:
            for s in (1, -1):
                for h in (0, 1):
                    self.copy(("a1", h, s)).wait_recv()
                    self.copy(("a2", h, s)).start()
            for s in (1, -1):
                for h in (0, 1):
                    for t in (1, -1):
                        self.copy(("b1", h, -s, t)).start()
                    self.across(h, self.off(h, -s)).start()
        if number == 1:
            for h in (0, 1):
                for s in (1, -1):
                    self.copy(("a2", h, s)).wait_recv()
                for t in (1, -1):
                    self.copy(("b1", h, 2, t)).start()
                self.across(h, self.off(h, 2)).start()
            for s in (1, -1):
                for h in (0, 1):
                    self.relay(h, 0, s)
        if number in (2, 3):
            for o in ((-1, 1), (2,))[number - 2]:
                for s in (1, -1):
                    for h in (0, 1):
                        self.relay(h, o, s)

    def share_last(self):
        for o in (0, -1, 1, 2):
            for h in (0, 1):
                for s in (1, -1):
                    self.copy(("b2", h, o, s)).wait_recv()
                self.across(h, self.off(h, o, 2)).start()

    def finish(self):
        for i in range(STEPS):
            for h in (0, 1):
                self.across(h, divmod(i, SIDE)).wait_recv()
        self.keep.wait()

    def drain(self):
        for i in range(STEPS):
            for h in (0, 1):
                self.across(h, divmod(i, SIDE)).wait_send()
        for key in self.keys:
            self.copy(key).wait_send()


class GatherRows:
    def __init__(self, place, own, buf, send, recv, side_send, side_recv, local):
        self.place, self.own, self.buf = place, own, buf
        self.sems, self.side_sems = (send, recv), (side_send, side_recv)
        self.keep = pltpu.make_async_copy(own, buf.at[place.q, place.core], local)
        self.order = sorted(range(1, STEPS), key=lambda i: -sum(min(k, SIDE - k) for k in divmod(i, SIDE)))

    def copy(self, i):
        place, (dy, dx) = self.place, divmod(i, SIDE)
        to = place.device(place.chip(dy, dx), place.core)
        return remote(self.own, self.buf.at[place.q, place.core], self.sems[0].at[i], self.sems[1].at[i], to)

    def across(self, i):
        place, (dy, dx) = self.place, divmod(i, SIDE)
        dst = self.buf.at[place.chip(-dy, -dx), place.core]
        return remote(dst if i else self.own, dst, self.side_sems[0].at[i], self.side_sems[1].at[i], place.partner)

    def begin(self):
        for i in self.order:
            self.copy(i).start()
        self.across(0).start()
        self.keep.start()

    def finish(self):
        for i in reversed(self.order):
            self.copy(i).wait_recv()
            self.across(i).start()
        for i in range(STEPS):
            self.across(i).wait_recv()
        self.keep.wait()

    def drain(self):
        for i in range(STEPS):
            self.across(i).wait_send()
        for i in self.order:
            self.copy(i).wait_send()


def turned(ref, i, start):
    return ref[i, pl.ds(start, LANE, stride=2), :].T


def kernel(blocks, rates, mask, gain_rows, watched, back_hbm, start_hbm, filt_rows, smooth_rows,
           gain, back, mid, back_rows, start_rows, woven, spread, obs, prior, filt, smooth,
           gains, backs, seen, kept, pmap, qmap, parts, stage, enter, leave, turn, far, near, sout, fsend,
           ksend, krecv, kside_s, kside_r, gsend, grecv, gside_s, gside_r,
           osend, orecv, msend, mrecv, mside_s, mside_r, chain, fsem, ssem, local):
    place = Place(blocks)
    core = place.core
    share = watched.shape[1] // (2 * STEPS)
    paths = watched.shape[1]
    barrier = pltpu.get_barrier_semaphore()
    greet = [place.partner, place.above(1), place.above(-1)]
    for i in range(1, STEPS):
        q = place.chip(*divmod(i, SIDE))
        greet += [place.device(q, core), place.device(q, 1 - core)]
    for device in greet:
        pl.semaphore_signal(barrier, inc=1, device_id=device, device_id_type=pl.DeviceIdType.MESH)
    loads = []
    for i in range(4):
        loads.append(pltpu.make_async_copy(back_hbm.at[:, pl.ds(i * LANE, LANE)], back_rows.at[i], local.at[5 + i]))
    for i in range(paths // LANE):
        loads.append(pltpu.make_async_copy(start_hbm.at[:, pl.ds(i * LANE, LANE)], start_rows.at[i], local.at[9 + i]))
    for load in loads:
        load.start()

    kept_gain = gain_rows[...] * mask[...].astype(F32)
    for i in (0, 1):
        mid[i, pl.ds(0, 2 * LANE), :] = kept_gain[:, i * LANE:(i + 1) * LANE]
        for comp in (0, 1):
            gain[i * LANE:(i + 1) * LANE, comp * LANE:(comp + 1) * LANE] = turned(mid, i, comp)
    pl.semaphore_wait(barrier, len(greet))
    first = Gather(place, gain, gains, ksend, krecv, kside_s, kside_r, local.at[1])
    second = Gather(place, back, backs, gsend, grecv, gside_s, gside_r, local.at[2])
    first.begin()

    for load in loads:
        load.wait()
    live = jnp.where(lax.axis_index("tm") == blocks * STEPS - 1, 0.0, 1.0).astype(F32)
    for comp in (0, 1):
        for i in range(4):
            mid[comp, pl.ds(i * LANE, LANE), :] = turned(back_rows, i, comp) * live
    first.stage(0)
    for block in range(4):
        begin = block // 2 * 2 * LANE + block % 2
        for comp in (0, 1):
            rows = mid[comp, pl.ds(begin, LANE, stride=2), :]
            back[pl.ds(block * LANE, LANE), pl.ds(comp * LANE, LANE)] = rows
    first.stage(1)

    sites = watched[...].T
    for i in range(2 * STEPS):
        obs[i // 2, i % 2] = sites[i * share:(i + 1) * share]
    watch = []
    for i in range(1, STEPS):
        q = place.chip(*divmod(i, SIDE))
        copy = remote(obs.at[q, core], seen.at[place.q], osend.at[i], orecv.at[i], place.device(q, core))
        copy.start()
        watch.append(copy)
    own_obs = pltpu.make_async_copy(obs.at[place.q, core], seen.at[place.q], local.at[0])
    own_obs.start()

    @pl.when(place.z == 0)
    def _():
        row = lax.broadcasted_iota(jnp.int32, (PAD, LANE), 0)
        lane = lax.broadcasted_iota(jnp.int32, (PAD, LANE), 1)
        for block in range(4):
            total = jnp.zeros((PAD, LANE), F32)
            for i in range(paths // LANE):
                wanted = lane + i * LANE == row + (place.q * 2 + core) * share
                pick = jnp.where(jnp.logical_and(wanted, row < share), 1.0, 0.0).astype(BF16)
                rest = start_rows[i, pl.ds(block // 2 * 2 * LANE + block % 2, LANE, stride=2), :]
                for _ in range(3):
                    part = rest.astype(BF16)
                    rest = rest - part.astype(F32)
                    total += lax.dot_general(pick, part, (((1,), (1,)), ((), ())), preferred_element_type=F32)
            prior[:, block * LANE:(block + 1) * LANE] = total

    @pl.when(place.z > 0)
    def _():
        prior[...] = jnp.zeros_like(prior)

    decay = jnp.exp(-rates[...])
    own = (decay * (1.0 + rates[...]), decay * (1.0 - rates[...]))
    other = (decay, -decay * rates[...] * rates[...])

    def ordered(pair):
        return jnp.concatenate([pair[comp][:, half * LANE:(half + 1) * LANE] for half in (0, 1) for comp in (0, 1)], 1)

    alpha, beta = ordered(own), ordered(other)
    first.stage(2)
    first.stage(3)
    second.begin()
    first.share_last()
    first.finish()
    for copy in watch:
        copy.wait_recv()
    own_obs.wait()

    def moved(state):
        swap = jnp.concatenate([state[:, i * LANE:(i + 1) * LANE] for i in (1, 0, 3, 2)], 1)
        return alpha * state + beta * swap

    def values(state):
        return jnp.concatenate([state[:, :LANE], state[:, 2 * LANE:3 * LANE]], 1)

    row = lax.broadcasted_iota(jnp.int32, (PAD, 4 * LANE), 0)
    lane = lax.broadcasted_iota(jnp.int32, (PAD, 4 * LANE), 1)
    unit = jnp.where(lane == row + (place.q * 2 + core) * PAD, 1.0, 0.0).astype(F32)
    zero = jnp.zeros((PAD, 4 * LANE), F32)
    last = blocks - 1

    def forward(k, state):
        predicted = moved(state)
        target = jnp.concatenate([seen[k], jnp.zeros((state.shape[0] - share, 2 * LANE), F32)], 0)
        innovation = target - values(predicted)
        state = predicted + jnp.concatenate([product(innovation, gains[k, half]) for half in (0, 1)], 1)
        kept[k] = state[:PAD]
        return state

    def whole(ref):
        state = jnp.concatenate([ref[0], ref[1]], 1)
        return jnp.concatenate([state, jnp.zeros((PAD - share, 4 * LANE), F32)], 0)

    def put(ref, state):
        for half in (0, 1):
            ref[half] = state[:share, half * 2 * LANE:(half + 1) * 2 * LANE]

    def parts_of(table):
        for q in range(STEPS):
            for i in (0, 1):
                high, low = halves(table[q, i])
                rows = pl.ds((q * 2 + i) * PAD, PAD)
                parts[0, rows, :] = high
                parts[1, rows, :] = low

    def hop(link, given, offset):
        dot = functools.partial(jnp.dot, preferred_element_type=F32)
        pair = []
        for half in (0, 1):
            link[half].wait_recv()
            value = jnp.concatenate([given[half], jnp.zeros((PAD - share, 2 * LANE), F32)], 0)
            high, low = halves(value)
            pair.append((high, jnp.concatenate([high, low], 0)))
        for half in (0, 1):
            lanes = pl.ds(half * 2 * LANE, 2 * LANE)
            total = offset[half]
            for part in (0, 1):
                rows = pl.ds(part * 2 * LANE, 2 * LANE)
                both = dot(pair[part][1], parts[0, rows, lanes])
                total += (both[:PAD] + (both[PAD:] + dot(pair[part][0], parts[1, rows, lanes])))[:share]
            offset[half] = total
            link[half].start()

    both = lax.fori_loop(0, STEPS, forward, jnp.concatenate([prior[...], unit], 0))
    put(leave, both)
    stage[...] = both[PAD:]
    up = [remote(leave.at[i], enter.at[i], chain.at[0, i], chain.at[1, i], place.above(1)) for i in (0, 1)]
    maps = GatherRows(place, stage, pmap, msend.at[0], mrecv.at[0], mside_s.at[0], mside_r.at[0], local.at[3])
    through = jnp.logical_and(place.z > DIRECT, place.z < last)

    @pl.when(place.z == 0)
    def _():
        for copy in up:
            copy.start()

    @pl.when(through)
    def _():
        maps.begin()

    second.stage(0)

    def filter_again():
        return lax.fori_loop(0, STEPS, forward, whole(enter))

    def entered():
        for copy in up:
            copy.wait_recv()

    def pass_on():
        entered()
        put(leave, filter_again())
        for copy in up:
            copy.start()

    @pl.when(jnp.logical_and(place.z > 0, place.z <= 2))
    def _():
        pass_on()

    @pl.when(through)
    def _():
        maps.finish()
        parts_of(pmap)

    second.stage(1)

    @pl.when(jnp.logical_or(place.z == 3, place.z == 4))
    def _():
        pass_on()

    second.stage(2)

    @pl.when(jnp.logical_and(place.z > 4, place.z <= DIRECT))
    def _():
        pass_on()

    second.stage(3)

    @pl.when(through)
    def _():
        hop(up, enter, leave)
        filter_again()

    second.share_last()

    @pl.when(place.z == last)
    def _():
        entered()
        filter_again()

    second.finish()

    def back_product(k, value):
        return jnp.concatenate([product(value, backs[k, half]) for half in (0, 1)], 1)

    def keep_smooth(k, state):
        put(sout.at[k], state)

    def both_back(i, state):
        k = STEPS - 1 - i
        held = kept[k]
        wanted = jnp.concatenate([state[:PAD] - moved(held), state[PAD:]], 0)
        state = jnp.concatenate([held, zero], 0) + back_product(k, wanted)
        keep_smooth(k, state[:PAD])
        return state

    @pl.when(jnp.logical_and(place.z > 0, place.z != last - 1))
    def _():
        both = lax.fori_loop(0, STEPS, both_back, jnp.concatenate([zero, unit], 0))
        turn[...] = both[PAD:]
        put(far, both)

    turns = GatherRows(place, turn, qmap, msend.at[1], mrecv.at[1], mside_s.at[1], mside_r.at[1], local.at[4])
    down = [remote(far.at[i], near.at[i], chain.at[2, i], chain.at[3, i], place.above(-1)) for i in (0, 1)]
    through = jnp.logical_and(place.z >= 1, place.z < last - 1)

    def hand_on(value_ref, k, out, sem):
        for half in (0, 1):
            part = value_ref.at[k, half]
            home = jnp.logical_and(k == place.q, core == half)

            @pl.when(home)
            def _():
                pltpu.make_async_copy(part, out.at[place.q, core], sem.at[1]).start()

            @pl.when(jnp.logical_not(home))
            def _():
                remote(part, out.at[place.q, core], sem.at[0], sem.at[1], place.device(k, half)).start()

    def hand_filtered(k, carry):
        put(fsend.at[k], kept[k])
        hand_on(fsend, k, filt, fsem)
        return carry

    def hand_smoothed(i, carry):
        hand_on(sout, STEPS - 1 - i, smooth, ssem)
        return carry

    def all_handed(out, sem):
        pltpu.make_async_copy(out, out, sem.at[1]).wait()
        rest = out.at[pl.ds(0, STEPS - 1)]
        pltpu.make_async_copy(rest, rest, sem.at[0]).wait()
        pltpu.make_async_copy(out.at[0, 0], out.at[0, 0], sem.at[0]).wait()

    def emit(table, rows):
        for i in range(2 * STEPS):
            spread[pl.ds(i * share, share), :] = table[i // 2, i % 2]
        for comp in (0, 1):
            for i in range(paths // LANE):
                block = spread[pl.ds(i * LANE, LANE), pl.ds(comp * LANE, LANE)]
                woven[i, pl.ds(comp, LANE, stride=2), :] = block.T
        for i in range(paths // LANE):
            rows[:, i * LANE:(i + 1) * LANE] = woven[i]

    def smooth_again():
        def step(i, state):
            k = STEPS - 1 - i
            state = kept[k] + back_product(k, state - moved(kept[k]))
            keep_smooth(k, state)
            hand_on(sout, k, smooth, ssem)
            return state

        return lax.fori_loop(0, STEPS, step, whole(near))

    @pl.when(place.z == last)
    def _():
        for copy in down:
            copy.start()

    @pl.when(through)
    def _():
        turns.begin()

    @pl.when(place.z == last - 1)
    def _():
        for copy in down:
            copy.wait_recv()
        put(far, smooth_again())
        for copy in down:
            copy.start()

    @pl.when(through)
    def _():
        turns.finish()
        parts_of(qmap)

    def hand_all_filtered():
        lax.fori_loop(0, STEPS, hand_filtered, 0)

    early = place.z < last // 2 + 1

    @pl.when(early)
    def _():
        hand_all_filtered()

    @pl.when(place.z < last // 2)
    def _():
        all_handed(filt, fsem)
        emit(filt, filt_rows)

    @pl.when(place.z == 0)
    def _():
        for copy in down:
            copy.wait_recv()

    @pl.when(through)
    def _():
        hop(down, near, far)

    @pl.when(jnp.logical_not(early))
    def _():
        hand_all_filtered()

    @pl.when(place.z == last)
    def _():
        lax.fori_loop(0, STEPS, hand_smoothed, 0)

    @pl.when(place.z < last - 1)
    def _():
        smooth_again()

    @pl.when(place.z >= last // 2)
    def _():
        all_handed(filt, fsem)
        emit(filt, filt_rows)

    @pl.when(place.z < last)
    def _():
        for copy in up:
            copy.wait_send()

    @pl.when(place.z > 0)
    def _():
        for copy in down:
            copy.wait_send()

    @pl.when(jnp.logical_and(place.z > DIRECT, place.z < last))
    def _():
        maps.drain()

    @pl.when(through)
    def _():
        turns.drain()

    first.drain()
    second.drain()
    for copy in watch:
        copy.wait_send()
    all_handed(smooth, ssem)
    emit(smooth, smooth_rows)


def body(site_rates, prior_mean, observed, obs_mask, filter_gains, smooth_gains):
    blocks = lax.axis_size("tm") // STEPS
    paths = prior_mean.shape[1]
    vmem, dma = pl.BlockSpec(memory_space=pltpu.VMEM), pltpu.SemaphoreType.DMA
    out = jax.ShapeDtypeStruct((2 * LANE, paths), F32)
    share = paths // (2 * STEPS)
    shared, chained = (STEPS, 2, share, 2 * LANE), (2, share, 2 * LANE)
    wide = (STEPS, 2, PAD, 4 * LANE)
    narrow = (PAD, 4 * LANE)
    sizes = [
        (2 * LANE, 2 * LANE), (4 * LANE, 2 * LANE), (2, 4 * LANE, LANE), (4, 2 * LANE, LANE),
        (paths // LANE, 4 * LANE, LANE), (paths // LANE, 2 * LANE, LANE), (paths, 2 * LANE), shared, narrow, shared, shared,
        (STEPS, 2, 2 * LANE, 2 * LANE), (STEPS, 2, 4 * LANE, 2 * LANE), (STEPS, share, 2 * LANE), (STEPS, PAD, 4 * LANE),
        wide, wide, (BF16, 2, 4 * LANE, 4 * LANE), narrow, chained, chained, narrow, chained, chained, shared, shared,
    ]
    filt, smooth = pl.pallas_call(
        functools.partial(kernel, blocks),
        out_shape=(out, out),
        in_specs=[vmem] * 4 + [pl.BlockSpec(memory_space=pl.ANY)] * 2,
        out_specs=(vmem, vmem),
        scratch_shapes=[pltpu.VMEM(size[-3:], BF16) if size[0] is BF16 else pltpu.VMEM(size, F32) for size in sizes] + [
            dma((40,)), dma((40,)), dma((32,)), dma((32,)),
            dma((40,)), dma((40,)), dma((32,)), dma((32,)),
            dma((STEPS,)), dma((STEPS,)),
            dma((2, STEPS)), dma((2, STEPS)), dma((2, STEPS)), dma((2, STEPS)),
            dma((4, 2)), dma((2,)), dma((2,)), dma((12,)),
        ],
        compiler_params=pltpu.CompilerParams(
            collective_id=0, has_side_effects=True, vmem_limit_bytes=60 * 1024 * 1024
        ),
        name="two_level_scan",
    )(site_rates[None], obs_mask, filter_gains[0], observed[0], smooth_gains[0], prior_mean)
    return filt[None], smooth[None]


def solution(mesh):
    placed = (
        P(),
        P(),
        P("tm", None, None),
        P("tm", None),
        P("tm", "rows", None),
        P("tm", "rows", None),
    )
    return jax.shard_map(
        body,
        mesh=mesh,
        in_specs=placed,
        out_specs=(P("tm", "rows", None), P("tm", "rows", None)),
        check_vma=False,
    )
```

```python
import functools

import jax
import jax.numpy as jnp
from jax import lax
from jax.experimental import pallas as pl
from jax.experimental.pallas import tpu as pltpu
from jax.sharding import PartitionSpec as P

F32, BF16 = jnp.float32, jnp.bfloat16
SIDE = 4
STEPS = SIDE * SIDE
LANE = 128
DIRECT = 5
PAD = 16


def halves(value):
    high = value.astype(BF16)
    return high, (value - high.astype(F32)).astype(BF16)


def product(left, right):
    dot = functools.partial(jnp.dot, preferred_element_type=F32)
    left_high, left_low = halves(left)
    right_high, right_low = halves(right)
    rows = left.shape[0]
    both = dot(jnp.concatenate([left_high, left_low], 0), right_high)
    return both[:rows] + (both[rows:] + dot(left_high, right_low))


class Place:
    def __init__(self, blocks):
        time = lax.axis_index("tm")
        self.blocks = blocks
        self.z, self.q = lax.div(time, STEPS), lax.rem(time, STEPS)
        self.y, self.x = lax.div(self.q, SIDE), lax.rem(self.q, SIDE)
        self.core = lax.axis_index("rows")
        self.partner = {"tm": time, "rows": 1 - self.core}

    def chip(self, dy, dx):
        return lax.rem(self.y + dy % SIDE, SIDE) * SIDE + lax.rem(self.x + dx % SIDE, SIDE)

    def device(self, q, core):
        return {"tm": self.z * STEPS + q, "rows": core}

    def above(self, dz):
        z = lax.rem(self.z + dz % self.blocks, self.blocks)
        return {"tm": z * STEPS + self.q, "rows": self.core}


def remote(src, dst, send, recv, device):
    return pltpu.make_async_remote_copy(
        src_ref=src, dst_ref=dst, send_sem=send, recv_sem=recv, device_id=device, device_id_type=pl.DeviceIdType.MESH
    )


class Gather:
    def __init__(self, place, own, buf, send, recv, side_send, side_recv, local):
        self.place, self.own, self.buf = place, own, buf
        self.half, self.quarter = own.shape[0] // 2, own.shape[0] // 4
        self.sems, self.side_sems = (send, recv), (side_send, side_recv)
        self.keep = pltpu.make_async_copy(own, buf.at[place.q, place.core], local)
        signs, sides = (1, -1), (0, 1)
        keys = [("a1", h, s) for h in sides for s in signs] + [("a2", h, s) for h in sides for s in signs]
        keys += [(name, h, o, s) for name in ("b1", "b2") for h in sides for o in (0, -1, 1, 2) for s in signs]
        self.keys = {key: i for i, key in enumerate(keys)}

    @staticmethod
    def off(h, along, across=0):
        return ((across, along), (along, across))[h]

    def copy(self, key):
        name, h, s = key[0], key[1], key[-1]
        start, size = h * self.half, self.half
        if name == "a1":
            offset, to = (0, 0), self.off(h, s)
        elif name == "a2":
            offset, to = self.off(h, -s), self.off(h, s)
        elif name == "b1":
            offset, to = self.off(h, key[2]), self.off(h, 0, s)
        else:
            offset, to = self.off(h, key[2], -s), self.off(h, 0, s)
        if name in ("a2", "b2"):
            start, size = start + (self.quarter if s < 0 else 0), self.quarter
        place, i = self.place, self.keys[key]
        dst = self.buf.at[place.chip(*offset), place.core, pl.ds(start, size)]
        src = self.own.at[pl.ds(start, size)] if offset == (0, 0) else dst
        return remote(src, dst, self.sems[0].at[i], self.sems[1].at[i], place.device(place.chip(*to), place.core))

    def across(self, h, offset):
        place, dy, dx = self.place, offset[0] % SIDE, offset[1] % SIDE
        i = h * STEPS + dy * SIDE + dx
        part = pl.ds(h * self.half, self.half)
        dst = self.buf.at[place.chip(dy, dx), place.core, part]
        src = self.own.at[part] if (dy, dx) == (0, 0) else dst
        return remote(src, dst, self.side_sems[0].at[i], self.side_sems[1].at[i], place.partner)

    def begin(self):
        for name, rest in (("a1", ()), ("b1", (0,))):
            for h in (0, 1):
                for s in (1, -1):
                    self.copy((name, h, *rest, s)).start()
        for h in (0, 1):
            self.across(h, (0, 0)).start()
        self.keep.start()

    def relay(self, h, o, s):
        self.copy(("b1", h, o, s)).wait_recv()
        self.copy(("b2", h, o, s)).start()
        self.across(h, self.off(h, o, -s)).start()

    def stage(self, number):
        if number == 0:
            for s in (1, -1):
                for h in (0, 1):
                    self.copy(("a1", h, s)).wait_recv()
                    self.copy(("a2", h, s)).start()
            for s in (1, -1):
                for h in (0, 1):
                    for t in (1, -1):
                        self.copy(("b1", h, -s, t)).start()
                    self.across(h, self.off(h, -s)).start()
        if number == 1:
            for h in (0, 1):
                for s in (1, -1):
                    self.copy(("a2", h, s)).wait_recv()
                for t in (1, -1):
                    self.copy(("b1", h, 2, t)).start()
                self.across(h, self.off(h, 2)).start()
            for s in (1, -1):
                for h in (0, 1):
                    self.relay(h, 0, s)
        if number in (2, 3):
            for o in ((-1, 1), (2,))[number - 2]:
                for s in (1, -1):
                    for h in (0, 1):
                        self.relay(h, o, s)

    def share_last(self):
        for o in (0, -1, 1, 2):
            for h in (0, 1):
                for s in (1, -1):
                    self.copy(("b2", h, o, s)).wait_recv()
                self.across(h, self.off(h, o, 2)).start()

    def finish(self):
        for i in range(STEPS):
            for h in (0, 1):
                self.across(h, divmod(i, SIDE)).wait_recv()
        self.keep.wait()

    def drain(self):
        for i in range(STEPS):
            for h in (0, 1):
                self.across(h, divmod(i, SIDE)).wait_send()
        for key in self.keys:
            self.copy(key).wait_send()


class GatherRows:
    def __init__(self, place, own, buf, send, recv, side_send, side_recv, local):
        self.place, self.own, self.buf = place, own, buf
        self.sems, self.side_sems = (send, recv), (side_send, side_recv)
        self.keep = pltpu.make_async_copy(own, buf.at[place.q, place.core], local)
        self.order = sorted(range(1, STEPS), key=lambda i: -sum(min(k, SIDE - k) for k in divmod(i, SIDE)))

    def copy(self, i):
        place, (dy, dx) = self.place, divmod(i, SIDE)
        to = place.device(place.chip(dy, dx), place.core)
        return remote(self.own, self.buf.at[place.q, place.core], self.sems[0].at[i], self.sems[1].at[i], to)

    def across(self, i):
        place, (dy, dx) = self.place, divmod(i, SIDE)
        dst = self.buf.at[place.chip(-dy, -dx), place.core]
        return remote(dst if i else self.own, dst, self.side_sems[0].at[i], self.side_sems[1].at[i], place.partner)

    def begin(self):
        for i in self.order:
            self.copy(i).start()
        self.across(0).start()
        self.keep.start()

    def finish(self):
        for i in reversed(self.order):
            self.copy(i).wait_recv()
            self.across(i).start()
        for i in range(STEPS):
            self.across(i).wait_recv()
        self.keep.wait()

    def drain(self):
        for i in range(STEPS):
            self.across(i).wait_send()
        for i in self.order:
            self.copy(i).wait_send()


def turned(ref, i, start):
    return ref[i, pl.ds(start, LANE, stride=2), :].T


def kernel(blocks, rates, mask, gain_rows, watched, back_hbm, start_hbm, filt_rows, smooth_rows,
           gain, back, mid, back_rows, start_rows, woven, spread, obs, prior, filt, smooth,
           gains, backs, seen, kept, pmap, qmap, parts, stage, enter, leave, turn, far, near, sout, fsend,
           ksend, krecv, kside_s, kside_r, gsend, grecv, gside_s, gside_r,
           osend, orecv, msend, mrecv, mside_s, mside_r, chain, fsem, ssem, local):
    place = Place(blocks)
    core = place.core
    share = watched.shape[1] // (2 * STEPS)
    paths = watched.shape[1]
    barrier = pltpu.get_barrier_semaphore()
    greet = [place.partner, place.above(1), place.above(-1)]
    for i in range(1, STEPS):
        q = place.chip(*divmod(i, SIDE))
        greet += [place.device(q, core), place.device(q, 1 - core)]
    for device in greet:
        pl.semaphore_signal(barrier, inc=1, device_id=device, device_id_type=pl.DeviceIdType.MESH)
    loads = []
    for i in range(4):
        loads.append(pltpu.make_async_copy(back_hbm.at[:, pl.ds(i * LANE, LANE)], back_rows.at[i], local.at[5 + i]))
    for i in range(paths // LANE):
        loads.append(pltpu.make_async_copy(start_hbm.at[:, pl.ds(i * LANE, LANE)], start_rows.at[i], local.at[9 + i]))
    for load in loads:
        load.start()

    kept_gain = gain_rows[...] * mask[...].astype(F32)
    for i in (0, 1):
        mid[i, pl.ds(0, 2 * LANE), :] = kept_gain[:, i * LANE:(i + 1) * LANE]
        for comp in (0, 1):
            gain[i * LANE:(i + 1) * LANE, comp * LANE:(comp + 1) * LANE] = turned(mid, i, comp)
    pl.semaphore_wait(barrier, len(greet))
    first = Gather(place, gain, gains, ksend, krecv, kside_s, kside_r, local.at[1])
    second = Gather(place, back, backs, gsend, grecv, gside_s, gside_r, local.at[2])
    first.begin()

    for load in loads:
        load.wait()
    live = jnp.where(lax.axis_index("tm") == blocks * STEPS - 1, 0.0, 1.0).astype(F32)
    for comp in (0, 1):
        for i in range(4):
            mid[comp, pl.ds(i * LANE, LANE), :] = turned(back_rows, i, comp) * live
    first.stage(0)
    for block in range(4):
        begin = block // 2 * 2 * LANE + block % 2
        for comp in (0, 1):
            rows = mid[comp, pl.ds(begin, LANE, stride=2), :]
            back[pl.ds(block * LANE, LANE), pl.ds(comp * LANE, LANE)] = rows
    first.stage(1)

    sites = watched[...].T
    for i in range(2 * STEPS):
        obs[i // 2, i % 2] = sites[i * share:(i + 1) * share]
    watch = []
    for i in range(1, STEPS):
        q = place.chip(*divmod(i, SIDE))
        copy = remote(obs.at[q, core], seen.at[place.q], osend.at[i], orecv.at[i], place.device(q, core))
        copy.start()
        watch.append(copy)
    own_obs = pltpu.make_async_copy(obs.at[place.q, core], seen.at[place.q], local.at[0])
    own_obs.start()

    @pl.when(place.z == 0)
    def _():
        row = lax.broadcasted_iota(jnp.int32, (PAD, LANE), 0)
        lane = lax.broadcasted_iota(jnp.int32, (PAD, LANE), 1)
        for block in range(4):
            total = jnp.zeros((PAD, LANE), F32)
            for i in range(paths // LANE):
                wanted = lane + i * LANE == row + (place.q * 2 + core) * share
                pick = jnp.where(jnp.logical_and(wanted, row < share), 1.0, 0.0).astype(BF16)
                rest = start_rows[i, pl.ds(block // 2 * 2 * LANE + block % 2, LANE, stride=2), :]
                for _ in range(3):
                    part = rest.astype(BF16)
                    rest = rest - part.astype(F32)
                    total += lax.dot_general(pick, part, (((1,), (1,)), ((), ())), preferred_element_type=F32)
            prior[:, block * LANE:(block + 1) * LANE] = total

    @pl.when(place.z > 0)
    def _():
        prior[...] = jnp.zeros_like(prior)

    decay = jnp.exp(-rates[...])
    own = (decay * (1.0 + rates[...]), decay * (1.0 - rates[...]))
    other = (decay, -decay * rates[...] * rates[...])

    def ordered(pair):
        return jnp.concatenate([pair[comp][:, half * LANE:(half + 1) * LANE] for half in (0, 1) for comp in (0, 1)], 1)

    alpha, beta = ordered(own), ordered(other)
    first.stage(2)
    first.stage(3)
    second.begin()
    first.share_last()
    first.finish()
    for copy in watch:
        copy.wait_recv()
    own_obs.wait()

    def moved(state):
        swap = jnp.concatenate([state[:, i * LANE:(i + 1) * LANE] for i in (1, 0, 3, 2)], 1)
        return alpha * state + beta * swap

    def values(state):
        return jnp.concatenate([state[:, :LANE], state[:, 2 * LANE:3 * LANE]], 1)

    row = lax.broadcasted_iota(jnp.int32, (PAD, 4 * LANE), 0)
    lane = lax.broadcasted_iota(jnp.int32, (PAD, 4 * LANE), 1)
    unit = jnp.where(lane == row + (place.q * 2 + core) * PAD, 1.0, 0.0).astype(F32)
    zero = jnp.zeros((PAD, 4 * LANE), F32)
    last = blocks - 1

    def forward(k, state):
        predicted = moved(state)
        target = jnp.concatenate([seen[k], jnp.zeros((state.shape[0] - share, 2 * LANE), F32)], 0)
        innovation = target - values(predicted)
        state = predicted + jnp.concatenate([product(innovation, gains[k, half]) for half in (0, 1)], 1)
        kept[k] = state[:PAD]
        return state

    def whole(ref):
        state = jnp.concatenate([ref[0], ref[1]], 1)
        return jnp.concatenate([state, jnp.zeros((PAD - share, 4 * LANE), F32)], 0)

    def put(ref, state):
        for half in (0, 1):
            ref[half] = state[:share, half * 2 * LANE:(half + 1) * 2 * LANE]

    def parts_of(table):
        for q in range(STEPS):
            for i in (0, 1):
                high, low = halves(table[q, i])
                rows = pl.ds((q * 2 + i) * PAD, PAD)
                parts[0, rows, :] = high
                parts[1, rows, :] = low

    def hop(link, given, offset):
        dot = functools.partial(jnp.dot, preferred_element_type=F32)
        totals = [offset[0], offset[1]]
        for part in (0, 1):
            link[part].wait_recv()
            value = jnp.concatenate([given[part], jnp.zeros((PAD - share, 2 * LANE), F32)], 0)
            high, low = halves(value)
            stacked = jnp.concatenate([high, low], 0)
            rows = pl.ds(part * 2 * LANE, 2 * LANE)
            for half in (0, 1):
                lanes = pl.ds(half * 2 * LANE, 2 * LANE)
                both = dot(stacked, parts[0, rows, lanes])
                totals[half] += (both[:PAD] + (both[PAD:] + dot(high, parts[1, rows, lanes])))[:share]
                if part:
                    offset[half] = totals[half]
                    link[half].start()

    both = lax.fori_loop(0, STEPS, forward, jnp.concatenate([prior[...], unit], 0))
    put(leave, both)
    stage[...] = both[PAD:]
    up = [remote(leave.at[i], enter.at[i], chain.at[0, i], chain.at[1, i], place.above(1)) for i in (0, 1)]
    maps = GatherRows(place, stage, pmap, msend.at[0], mrecv.at[0], mside_s.at[0], mside_r.at[0], local.at[3])
    through = jnp.logical_and(place.z > DIRECT, place.z < last)

    @pl.when(place.z == 0)
    def _():
        for copy in up:
            copy.start()

    @pl.when(through)
    def _():
        maps.begin()

    second.stage(0)

    def filter_again():
        return lax.fori_loop(0, STEPS, forward, whole(enter))

    def entered():
        for copy in up:
            copy.wait_recv()

    def pass_on():
        entered()
        put(leave, filter_again())
        for copy in up:
            copy.start()

    @pl.when(jnp.logical_and(place.z > 0, place.z <= 2))
    def _():
        pass_on()

    @pl.when(through)
    def _():
        maps.finish()
        parts_of(pmap)

    second.stage(1)

    @pl.when(jnp.logical_or(place.z == 3, place.z == 4))
    def _():
        pass_on()

    second.stage(2)

    @pl.when(jnp.logical_and(place.z > 4, place.z <= DIRECT))
    def _():
        pass_on()

    second.stage(3)

    @pl.when(through)
    def _():
        hop(up, enter, leave)
        filter_again()

    second.share_last()

    @pl.when(place.z == last)
    def _():
        entered()
        filter_again()

    second.finish()

    def back_product(k, value):
        return jnp.concatenate([product(value, backs[k, half]) for half in (0, 1)], 1)

    def keep_smooth(k, state):
        put(sout.at[k], state)

    def both_back(i, state):
        k = STEPS - 1 - i
        held = kept[k]
        wanted = jnp.concatenate([state[:PAD] - moved(held), state[PAD:]], 0)
        state = jnp.concatenate([held, zero], 0) + back_product(k, wanted)
        keep_smooth(k, state[:PAD])
        return state

    @pl.when(jnp.logical_and(place.z > 0, place.z != last - 1))
    def _():
        both = lax.fori_loop(0, STEPS, both_back, jnp.concatenate([zero, unit], 0))
        turn[...] = both[PAD:]
        put(far, both)

    turns = GatherRows(place, turn, qmap, msend.at[1], mrecv.at[1], mside_s.at[1], mside_r.at[1], local.at[4])
    down = [remote(far.at[i], near.at[i], chain.at[2, i], chain.at[3, i], place.above(-1)) for i in (0, 1)]
    through = jnp.logical_and(place.z >= 1, place.z < last - 1)

    def hand_on(value_ref, k, out, sem):
        for half in (0, 1):
            part = value_ref.at[k, half]
            home = jnp.logical_and(k == place.q, core == half)

            @pl.when(home)
            def _():
                pltpu.make_async_copy(part, out.at[place.q, core], sem.at[1]).start()

            @pl.when(jnp.logical_not(home))
            def _():
                remote(part, out.at[place.q, core], sem.at[0], sem.at[1], place.device(k, half)).start()

    def hand_filtered(k, carry):
        put(fsend.at[k], kept[k])
        hand_on(fsend, k, filt, fsem)
        return carry

    def hand_smoothed(i, carry):
        hand_on(sout, STEPS - 1 - i, smooth, ssem)
        return carry

    def all_handed(out, sem):
        pltpu.make_async_copy(out, out, sem.at[1]).wait()
        rest = out.at[pl.ds(0, STEPS - 1)]
        pltpu.make_async_copy(rest, rest, sem.at[0]).wait()
        pltpu.make_async_copy(out.at[0, 0], out.at[0, 0], sem.at[0]).wait()

    def emit(table, rows):
        for i in range(2 * STEPS):
            spread[pl.ds(i * share, share), :] = table[i // 2, i % 2]
        for comp in (0, 1):
            for i in range(paths // LANE):
                block = spread[pl.ds(i * LANE, LANE), pl.ds(comp * LANE, LANE)]
                woven[i, pl.ds(comp, LANE, stride=2), :] = block.T
        for i in range(paths // LANE):
            rows[:, i * LANE:(i + 1) * LANE] = woven[i]

    def smooth_again():
        def step(i, state):
            k = STEPS - 1 - i
            state = kept[k] + back_product(k, state - moved(kept[k]))
            keep_smooth(k, state)
            hand_on(sout, k, smooth, ssem)
            return state

        return lax.fori_loop(0, STEPS, step, whole(near))

    @pl.when(place.z == last)
    def _():
        for copy in down:
            copy.start()

    @pl.when(through)
    def _():
        turns.begin()

    @pl.when(place.z == last - 1)
    def _():
        for copy in down:
            copy.wait_recv()
        put(far, smooth_again())
        for copy in down:
            copy.start()

    @pl.when(through)
    def _():
        turns.finish()
        parts_of(qmap)

    def hand_all_filtered():
        lax.fori_loop(0, STEPS, hand_filtered, 0)

    early = place.z < last // 2 + 1

    @pl.when(early)
    def _():
        hand_all_filtered()

    @pl.when(place.z < last // 2)
    def _():
        all_handed(filt, fsem)
        emit(filt, filt_rows)

    @pl.when(place.z == 0)
    def _():
        for copy in down:
            copy.wait_recv()

    @pl.when(through)
    def _():
        hop(down, near, far)

    @pl.when(jnp.logical_not(early))
    def _():
        hand_all_filtered()

    @pl.when(place.z == last)
    def _():
        lax.fori_loop(0, STEPS, hand_smoothed, 0)

    @pl.when(place.z < last - 1)
    def _():
        smooth_again()

    @pl.when(place.z >= last // 2)
    def _():
        all_handed(filt, fsem)
        emit(filt, filt_rows)

    @pl.when(place.z < last)
    def _():
        for copy in up:
            copy.wait_send()

    @pl.when(place.z > 0)
    def _():
        for copy in down:
            copy.wait_send()

    @pl.when(jnp.logical_and(place.z > DIRECT, place.z < last))
    def _():
        maps.drain()

    @pl.when(through)
    def _():
        turns.drain()

    first.drain()
    second.drain()
    for copy in watch:
        copy.wait_send()
    all_handed(smooth, ssem)
    emit(smooth, smooth_rows)


def body(site_rates, prior_mean, observed, obs_mask, filter_gains, smooth_gains):
    blocks = lax.axis_size("tm") // STEPS
    paths = prior_mean.shape[1]
    vmem, dma = pl.BlockSpec(memory_space=pltpu.VMEM), pltpu.SemaphoreType.DMA
    out = jax.ShapeDtypeStruct((2 * LANE, paths), F32)
    share = paths // (2 * STEPS)
    shared, chained = (STEPS, 2, share, 2 * LANE), (2, share, 2 * LANE)
    wide = (STEPS, 2, PAD, 4 * LANE)
    narrow = (PAD, 4 * LANE)
    sizes = [
        (2 * LANE, 2 * LANE), (4 * LANE, 2 * LANE), (2, 4 * LANE, LANE), (4, 2 * LANE, LANE),
        (paths // LANE, 4 * LANE, LANE), (paths // LANE, 2 * LANE, LANE), (paths, 2 * LANE), shared, narrow, shared, shared,
        (STEPS, 2, 2 * LANE, 2 * LANE), (STEPS, 2, 4 * LANE, 2 * LANE), (STEPS, share, 2 * LANE), (STEPS, PAD, 4 * LANE),
        wide, wide, (BF16, 2, 4 * LANE, 4 * LANE), narrow, chained, chained, narrow, chained, chained, shared, shared,
    ]
    filt, smooth = pl.pallas_call(
        functools.partial(kernel, blocks),
        out_shape=(out, out),
        in_specs=[vmem] * 4 + [pl.BlockSpec(memory_space=pl.ANY)] * 2,
        out_specs=(vmem, vmem),
        scratch_shapes=[pltpu.VMEM(size[-3:], BF16) if size[0] is BF16 else pltpu.VMEM(size, F32) for size in sizes] + [
            dma((40,)), dma((40,)), dma((32,)), dma((32,)),
            dma((40,)), dma((40,)), dma((32,)), dma((32,)),
            dma((STEPS,)), dma((STEPS,)),
            dma((2, STEPS)), dma((2, STEPS)), dma((2, STEPS)), dma((2, STEPS)),
            dma((4, 2)), dma((2,)), dma((2,)), dma((12,)),
        ],
        compiler_params=pltpu.CompilerParams(
            collective_id=0, has_side_effects=True, vmem_limit_bytes=60 * 1024 * 1024
        ),
        name="two_level_scan",
    )(site_rates[None], obs_mask, filter_gains[0], observed[0], smooth_gains[0], prior_mean)
    return filt[None], smooth[None]


def solution(mesh):
    placed = (
        P(),
        P(),
        P("tm", None, None),
        P("tm", None),
        P("tm", "rows", None),
        P("tm", "rows", None),
    )
    return jax.shard_map(
        body,
        mesh=mesh,
        in_specs=placed,
        out_specs=(P("tm", "rows", None), P("tm", "rows", None)),
        check_vma=False,
    )
```
